32 devices in a mesh: group: 2 (over x), wide: 8 (over z, y), narrow: 2 (over core).
Axes of the slice: x: 2, y: 2, z: 4, core: 2. Of those that a mesh axis runs over, the one named last changes fastest.
Arguments:
- voxels: bfloat16 [65536, 512], P(('group', 'wide', 'narrow')), parts along dimension 0, may hold values from -6 to 6
- w_qkv: bfloat16 [512, 1536], replicated, may hold values from -0.25 to 0.25
- w_out: bfloat16 [512, 512], replicated, may hold values from -0.25 to 0.25
- w_feature: bfloat16 [512, 256], replicated, may hold values from -0.25 to 0.25
- conv_first: bfloat16 [3, 3, 256, 256], replicated, may hold values from -0.125 to 0.125
- conv_second: bfloat16 [3, 3, 256, 256], replicated, may hold values from -0.125 to 0.125
- row_brick: int32 [512, 1], P(('group', 'wide', 'narrow')), parts along dimension 0, may hold values from 0 to 7; in each aligned block of 16 rows (0 to 15, 16 to 31, ...) at most 4 rows name the same one
- cell_place: int32 [65536], P(('group', 'wide', 'narrow')), parts along dimension 0, may hold values from 0 to 255
Outputs:
- flow_field: float32 [128, 64, 256], P(('group', 'wide'), 'narrow'), parts along dimension 0
The draws below stay inside these ranges and needn't reach their ends.
There are 2 independent parts, one for each index of `group`. The reference program is written for one: setup_inputs(seed, part) draws one part's arguments, and reference() takes and returns one part's arrays. A program takes and returns all parts, laid end to end along the dimension named above; an argument that names none is the same for every part. Nothing has to cross between parts.
Inputs may be any that keep to these rules, and one draw needn't show every extreme that they name: `row_brick`: within the rows of one device (16 rows in a row), no brick row is named more than 4 times, and some brick row exactly 4 times.
All inputs are finite; a program needn't handle non-finite values.
Results may differ from the reference program's by a relative error of at most 0.014.
Values may be sent and summed in bfloat16 or wider, within the bound.
A program may use at most 128 MiB of HBM per device.

```python
import math
import jax
import jax.numpy as jnp
import numpy as np
from jax import lax

D = 512
HEADS = 4
HEAD = 128
PF = 256
ROW = 128
BLK = 256
TOK_DEV = 2048
BX = 8
BY = 32
MOST = 4
TOKENS = 32768
ROWS = 256
N_WIDE = 8
N_NARROW = 2


def touch_ends(entries, rng, smallest, largest):
    extent = entries.shape
    spot = [jax.random.randint(jax.random.fold_in(rng, axis), (), 0, extent[axis]) for axis in range(len(extent))]
    entries = entries.at[tuple(spot)].set(smallest)
    longest = extent.index(max(extent))
    spot[longest] = (spot[longest] + 1) % extent[longest]
    return entries.at[tuple(spot)].set(largest)


def block_scale(key, dims, split, low, largest):
    factor_of, own = 1.0, jax.random.fold_in(key, 6)
    for position, parts in split:
        draws = jnp.exp(jax.random.uniform(jax.random.fold_in(own, position), (parts,), jnp.float32, low / len(split), largest / len(split)))
        factor_of = factor_of * jnp.repeat(draws, dims[position] // parts).reshape([-1 if axis == position else 1 for axis in range(len(dims))])
    return factor_of


def routed_block(stream_key, own, number, rows, count, top, reach, lean):
    sequence = jax.random.permutation(stream_key, count)
    packed, usual = load_shares(count, rows * top, reach, lean, True), load_shares(count, rows * top, reach, lean, False)
    places = jnp.arange(count)

    def named(sizes, offset_by):
        used = int((sizes > 0).sum())
        fixed = max(1, used // 4)
        passed = fixed + (places - fixed + offset_by * (used - fixed)) % max(1, count - fixed)
        return jnp.zeros((count,), jnp.int32).at[sequence[jnp.where(places < fixed, places, passed)]].set(jnp.asarray(sizes, jnp.int32))

    sizes = jnp.where(number % 4 == 0, named(packed, number // 4), named(usual, number - number // 4 - 1))
    mixed = jax.random.permutation(jax.random.fold_in(own, 3), count)
    donor, sink = mixed[0:count // 2 * 2:2], mixed[1:count // 2 * 2:2]
    margin = jnp.minimum(sizes[donor] - 1, reach - sizes[sink]) // 2
    margin = jnp.where((donor == sequence[0]) | (sink == sequence[0]) | (sizes[sink] == 0), 0, jnp.maximum(margin, 0))
    passed = jax.random.randint(jax.random.fold_in(own, 4), (count // 2,), 0, 1 << 20) % (margin + 1)
    sizes = sizes.at[donor].add(-passed).at[sink].add(passed)
    members = jnp.searchsorted(jnp.cumsum(sizes), jnp.arange(rows * top), side="right").astype(jnp.int32)
    grid = members.reshape(top, rows).T
    grid = grid[jax.random.permutation(jax.random.fold_in(own, 1), rows)]
    offset_by = jax.random.randint(jax.random.fold_in(own, 2), (rows, 1), 0, top)
    return jnp.take_along_axis(grid, (jnp.arange(top)[None, :] + offset_by) % top, axis=1)


def load_shares(count, total, limit, lean, full):
    weights = [(1 << 20) // math.isqrt(rank ** lean) + 1 for rank in range(1, count + 1)]
    largest = limit if full else min(limit, max(-(-total // count), total * weights[0] // sum(weights)))
    least = 1 if total - largest >= count - 1 else 0
    holding, spare = [largest] + [least] * (count - 1), total - largest - least * (count - 1)
    while spare > 0:
        free = [i for i in range(1, count) if holding[i] < largest] or [i for i in range(1, count) if holding[i] < limit]
        mass, left = sum([weights[i] for i in free]), spare
        for i in free:
            more = min(limit - holding[i], max(1, left * weights[i] // mass), spare)
            holding[i] = holding[i] + more
            spare = spare - more
    return np.array(holding)


def bell_draw(own_key, extent, scale, reach, split=(), held_as=jnp.bfloat16):
    result = jax.random.normal(own_key, extent, jnp.float32) * scale
    if len(split) > 0:
        result = block_scale(own_key, extent, split, -0.22, 0.18) * result
    return jnp.clip(result, min=-reach, max=reach).astype(held_as)


def setup_inputs(seed: int = 0, part: int = 0) -> dict:
    splits = jax.random.split(jax.random.key(seed), 9)
    part_splits = jax.random.split(jax.random.fold_in(splits[8], part), 9)
    voxels = bell_draw(part_splits[0], (TOKENS, D), 1.0, 6.0, ((0, 16),))
    w_qkv = bell_draw(splits[1], (D, 3 * D), D ** -0.5, 0.25)
    w_out = bell_draw(splits[2], (D, D), D ** -0.5, 0.25)
    w_feature = bell_draw(splits[3], (D, PF), D ** -0.5, 0.25)
    conv_first = bell_draw(splits[4], (3, 3, PF, PF), (9 * PF) ** -0.5, 0.125)
    conv_second = bell_draw(splits[5], (3, 3, PF, PF), (9 * PF) ** -0.5, 0.125)
    row_brick_keys = jax.random.split(jax.random.fold_in(part_splits[6], 1), ROWS // (TOK_DEV // ROW))
    row_brick_turns = jax.random.permutation(jax.random.fold_in(part_splits[6], 3), ROWS // (TOK_DEV // ROW))
    row_brick = jax.vmap(lambda own, number: routed_block(jax.random.fold_in(part_splits[6], 2), own, number, TOK_DEV // ROW, N_WIDE, 1, MOST, 2))(row_brick_keys, row_brick_turns).reshape((ROWS, 1))
    cell_place = touch_ends(jax.random.randint(part_splits[7], (TOKENS,), 0, BX * BY), jax.random.fold_in(part_splits[7], 1), 0, (BX * BY) - 1).astype(jnp.int32)
    return {"voxels": voxels, "w_qkv": w_qkv, "w_out": w_out, "w_feature": w_feature, "conv_first": conv_first, "conv_second": conv_second, "row_brick": row_brick, "cell_place": cell_place}


epsilon = 1e-06
layout_names = ('NHWC', 'HWIO', 'NHWC')

def convolve_same(field, weight):
    return lax.conv_general_dilated(field[None], weight, (1, 1), 'SAME', dimension_numbers=layout_names, preferred_element_type=jnp.float32)[0]

def reference(voxels, w_qkv, w_out, w_feature, conv_first, conv_second, row_brick, cell_place):
    projected = jnp.dot(voxels, w_qkv, preferred_element_type=jnp.float32).astype(jnp.bfloat16)
    block_count = TOKENS // BLK
    split_rows = projected.reshape(block_count, BLK, 3, HEADS, HEAD)
    query_rows = split_rows[:, :, 0]
    key_rows = split_rows[:, :, 1]
    value_rows = split_rows[:, :, 2]
    causal_mask = jnp.arange(BLK)[:, None] >= jnp.arange(BLK)[None, :]

    def advance(carry_state, block):
        query_block, key_block, value_block = block
        query_wide = query_block.astype(jnp.float32)
        key_wide = key_block.astype(jnp.float32)
        value_wide = value_block.astype(jnp.float32)
        carried = jnp.einsum('thd,hde->the', query_wide, carry_state, precision=lax.Precision.HIGHEST)
        scores = jnp.einsum('thd,shd->hts', query_wide, key_wide)
        scores = jnp.where(causal_mask[None], scores, 0.0).astype(jnp.bfloat16)
        local_part = jnp.einsum('hts,she->the', scores.astype(jnp.float32), value_wide)
        carry_state = carry_state + jnp.einsum('shd,she->hde', key_wide, value_wide)
        return (carry_state, carried + local_part)
    start_state = jnp.zeros((HEADS, HEAD, HEAD), jnp.float32)
    final_state, attended = lax.scan(advance, start_state, (query_rows, key_rows, value_rows))
    attended = attended.reshape(TOKENS, HEADS, HEAD)
    mean_square = lax.optimization_barrier(jnp.mean(attended * attended, axis=-1, keepdims=True))
    normed = (attended * lax.rsqrt(mean_square + epsilon)).astype(jnp.bfloat16).reshape(TOKENS, D)
    hidden = (voxels.astype(jnp.float32) + jnp.dot(normed, w_out, preferred_element_type=jnp.float32)).astype(jnp.bfloat16)
    features = jnp.dot(hidden, w_feature, preferred_element_type=jnp.float32).astype(jnp.bfloat16)
    row_index = jnp.arange(TOKENS, dtype=jnp.int32) // ROW
    column_brick = row_index // (TOK_DEV // ROW) % N_NARROW
    brick_index = row_brick[:, 0][row_index]
    grid_row = brick_index * BX + cell_place // BY
    grid_column = column_brick * BY + cell_place % BY
    flat_cell = (grid_row * (BY * N_NARROW) + grid_column).astype(jnp.int32)
    pooled = jax.ops.segment_sum(features.astype(jnp.float32), flat_cell, num_segments=BX * N_WIDE * BY * N_NARROW)
    pooled = pooled.astype(jnp.bfloat16).reshape(BX * N_WIDE, BY * N_NARROW, PF)
    inner_field = jax.nn.gelu(convolve_same(pooled, conv_first), approximate=True).astype(jnp.bfloat16)
    return convolve_same(inner_field, conv_second)
```

```python
import functools
import math

import jax
import jax.numpy as jnp
from jax import lax
from jax.experimental import pallas as pl
from jax.experimental.pallas import tpu as pltpu
from jax.sharding import PartitionSpec as P

D = 512
HEADS = 4
HEAD = 128
PF = 256
ROW = 128
BLK = 256
BX = 8
BY = 32
CELLS = BX * BY
PAIR = 2 * HEAD
EDGE = 16
WIDTH = BY + 2 * EDGE
HALO = 2
PIECES = 4
PIECE = CELLS // PIECES
PIECE_ORDER = (0, 3, 1, 2)
SWAPPED = 2
PARTS = 2
PART = HEAD // PARTS

epsilon = 1e-06
MESH = pl.DeviceIdType.MESH
F32 = jnp.float32
BF16 = jnp.bfloat16


def dot(a, b):
    return jnp.dot(a, b, preferred_element_type=F32)


def dot_t(a, b):
    return lax.dot_general(a, b, (((0,), (0,)), ((), ())), preferred_element_type=F32)


def dot_nt(a, b):
    return lax.dot_general(a, b, (((1,), (1,)), ((), ())), preferred_element_type=F32)


def diagonal(upper, lower):
    blank_right = jnp.zeros((upper.shape[0], lower.shape[1]), upper.dtype)
    blank_left = jnp.zeros((lower.shape[0], upper.shape[1]), lower.dtype)
    return jnp.concatenate(
        [
            jnp.concatenate([upper, blank_right], axis=1),
            jnp.concatenate([blank_left, lower], axis=1),
        ],
        axis=0,
    )


def swap_bits(label):
    return label - label % 4 + 2 * (label % 2) + (label // 2) % 2


def kernel(
    wide_count, narrow_count, token_count, most,
    vox_hbm, wqkv_hbm, wout_hbm, wfeat_hbm, first_hbm, second_hbm, brick_ref, cell_ref,
    out_ref,
    vox, wqkv, wout, wfeat, first, second,
    kv, qs, att, direct, mixed, within, total, feats, slots,
    own_total, quad_parts, quad_send, quad_recv, prefix_send, prefix_recv,
    part_send, part_recv, own_part,
    pooled, ext, rows_recv, cols_recv, corner_recv, inner,
    vox_sem, load_sem,
    s1, r1, s2, r2, s3, r3, sa, ra, sh, rh,
):
    blocks = token_count // BLK
    rows = token_count // ROW
    quads = wide_count // 2
    bits = wide_count.bit_length() - 1
    wide = lax.axis_index("wide")
    narrow = lax.axis_index("narrow")
    side = wide % 2
    quad = wide // 2
    members = 2 * narrow_count
    place = side * narrow_count + narrow

    def load_vox(b):
        span = pl.ds(pl.multiple_of(b * BLK, BLK), BLK)
        return pltpu.make_async_copy(vox_hbm.at[span], vox.at[span], vox_sem.at[b])

    def load(source, target, k):
        return pltpu.make_async_copy(source, target, load_sem.at[k])

    loads = [
        load(wqkv_hbm.at[:, pl.ds(D, 2 * D)], wqkv.at[:, pl.ds(D, 2 * D)], 0),
        load(wout_hbm, wout, 1),
        load(wfeat_hbm, wfeat, 2),
        load(first_hbm, first, 3),
        load(second_hbm, second, 4),
        load(wqkv_hbm.at[:, pl.ds(0, D)], wqkv.at[:, pl.ds(0, D)], 5),
    ]
    loads[0].start()
    for b in range(blocks):
        load_vox(b).start()
    for k in (5, 2, 1, 3, 4):
        loads[k].start()

    everyone = wide_count * narrow_count
    me = wide * narrow_count + narrow
    barrier = pltpu.get_barrier_semaphore()

    def greet(k, carry):
        other = (me + k) % everyone
        pl.semaphore_signal(
            barrier, inc=1,
            device_id={"wide": other // narrow_count, "narrow": other % narrow_count},
            device_id_type=MESH,
        )
        return carry

    lax.fori_loop(1, everyone, greet, 0)

    def remote(source, target, send_sem, recv_sem, to_wide, to_narrow):
        return pltpu.make_async_remote_copy(
            src_ref=source, dst_ref=target, send_sem=send_sem, recv_sem=recv_sem,
            device_id={"wide": to_wide, "narrow": to_narrow}, device_id_type=MESH,
        )

    causal = lax.broadcasted_iota(jnp.int32, (ROW, PAIR), 0) >= (
        lax.broadcasted_iota(jnp.int32, (ROW, PAIR), 1) % ROW
    )
    total[...] = jnp.zeros_like(total)
    ext[...] = jnp.zeros_like(ext)
    loads[0].wait()

    def keys_values(b, carry):
        load_vox(b).wait()
        span = pl.ds(pl.multiple_of(b * BLK, BLK), BLK)
        both = dot(vox[span, :], wqkv[:, D:]).astype(BF16)
        kv[span, :] = both
        for h in range(HEADS):
            key = both[:, h * HEAD:(h + 1) * HEAD]
            value = both[:, D + h * HEAD:D + (h + 1) * HEAD]
            state = dot_t(key, diagonal(value[:ROW], value[ROW:]))
            before = total[h]
            within[2 * b, h] = before.astype(BF16)
            middle = before + state[:, :HEAD]
            within[2 * b + 1, h] = middle.astype(BF16)
            total[h] = middle + state[:, HEAD:]
        return carry

    lax.fori_loop(0, blocks, keys_values, 0, unroll=4)

    for h in range(HEADS):
        own_total[h] = total[h].astype(BF16)
    pl.semaphore_wait(barrier, everyone - 1)

    def part_rows(j):
        return pl.ds(j * PART, PART)

    def member(t):
        other = (place + t) % members
        return other, quad * 2 + other // narrow_count, other % narrow_count

    def gather_copy(t, j):
        other, to_wide, to_narrow = member(t)
        return remote(
            own_total.at[other, part_rows(j)], quad_parts.at[t - 1, part_rows(j)],
            s1.at[t - 1, j], r1.at[t - 1, j], to_wide, to_narrow,
        )

    for j in range(PARTS):
        for t in range(1, members):
            gather_copy(t, j).start()

    def local(b, carry):
        span = pl.ds(pl.multiple_of(b * BLK, BLK), BLK)
        query = dot(vox[span, :], wqkv[:, :D]).astype(BF16)
        qs[span, :] = query
        direct[span, :] = dot(vox[span, :], wfeat[...])
        for c in range(BLK // ROW):
            chunk = pl.ds(pl.multiple_of(b * BLK + c * ROW, ROW), ROW)
            for p in range(HEADS // 2):
                columns = slice(p * PAIR, (p + 1) * PAIR)
                low, high = 2 * p * HEAD, (2 * p + 1) * HEAD
                keys = diagonal(kv[chunk, low:low + HEAD], kv[chunk, high:high + HEAD])
                scores = dot_nt(query[c * ROW:(c + 1) * ROW, columns], keys)
                scores = jnp.where(causal, scores, 0.0).astype(BF16)
                values = diagonal(
                    kv[chunk, D + low:D + low + HEAD], kv[chunk, D + high:D + high + HEAD]
                )
                att[chunk, columns] = dot(scores, values)
        return carry

    cut = blocks // 2
    loads[5].wait()
    loads[2].wait()
    lax.fori_loop(0, cut, local, 0, unroll=2)

    def later_copy(t, j):
        return remote(
            quad_send.at[part_rows(j)], quad_recv.at[t - 1, part_rows(j)],
            s2.at[t - 1, j], r2.at[t - 1, j],
            ((quad + t) % quads) * 2 + side, narrow,
        )

    for j in range(PARTS):
        piece = slice(j * PART, (j + 1) * PART)
        for t in range(1, members):
            gather_copy(t, j).wait_recv()
        quad_sum = own_total[place, piece].astype(F32)
        for t in range(1, members):
            quad_sum = quad_sum + quad_parts[t - 1, piece].astype(F32)
        quad_send[piece] = quad_sum.astype(BF16)
        for t in range(1, quads):
            @pl.when(quad + t < quads)
            def _(t=t, j=j):
                later_copy(t, j).start()

    lax.fori_loop(cut, blocks, local, 0, unroll=2)
    loads[1].wait()
    mixed[...] = dot(wout[...], wfeat[...]).astype(BF16)

    def assign(b, carry):
        held = [jnp.int32(-1)] * most
        for r in range(rows):
            hit = brick_ref[0, r] == b
            held = [
                jnp.where(hit, jnp.int32(r) if m == 0 else held[m - 1], held[m]) for m in range(most)
            ]
        for m in range(most):
            slots[b * most + m] = held[m]
        return carry

    lax.fori_loop(0, wide_count, assign, 0)

    def spread_copy(t, j):
        other, to_wide, to_narrow = member(t)
        return remote(
            prefix_send.at[other, part_rows(j)], prefix_recv.at[place, part_rows(j)],
            s3.at[t - 1, j], r3.at[t - 1, j], to_wide, to_narrow,
        )

    def spread_arrival(t, j):
        source = (place - t + members) % members
        return remote(
            prefix_send.at[source, part_rows(j)], prefix_recv.at[source, part_rows(j)],
            s3.at[t - 1, j], r3.at[t - 1, j], wide, narrow,
        )

    for j in range(PARTS):
        piece = slice(j * PART, (j + 1) * PART)
        total[0, piece] = jnp.zeros((PART, HEAD), F32)
        for t in range(1, quads):
            @pl.when(quad - t >= 0)
            def _(t=t, j=j, piece=piece):
                later_copy(t, j).wait_recv()
                total[0, piece] = total[0, piece] + quad_recv[t - 1, piece].astype(F32)
        running = total[0, piece]
        for m in range(members):
            prefix_send[m, piece] = running.astype(BF16)
            if m < members - 1:
                value = own_total[place, piece].astype(F32)
                for t in range(1, members):
                    value = jnp.where(
                        (place - t + members) % members == m,
                        quad_parts[t - 1, piece].astype(F32), value,
                    )
                running = running + value
        for t in range(1, members):
            spread_copy(t, j).start()
        prefix_recv[place, piece] = prefix_send[place, piece]

    for j in range(PARTS):
        for t in range(1, members):
            spread_arrival(t, j).wait_recv()
    for h in range(HEADS):
        total[h] = prefix_recv[h].astype(F32)

    def project(b, carry):
        normed = []
        for c in range(BLK // ROW):
            chunk = pl.ds(pl.multiple_of(b * BLK + c * ROW, ROW), ROW)
            pieces = []
            for p in range(HEADS // 2):
                columns = slice(p * PAIR, (p + 1) * PAIR)
                state = [
                    (within[2 * b + c, 2 * p + i].astype(F32) + total[2 * p + i]).astype(BF16)
                    for i in range(2)
                ]
                attended = att[chunk, columns] + dot(qs[chunk, columns], diagonal(*state))
                for i in range(2):
                    one = attended[:, i * HEAD:(i + 1) * HEAD]
                    square = jnp.mean(one * one, axis=-1, keepdims=True)
                    pieces.append((one * lax.rsqrt(square + epsilon)).astype(BF16))
            normed.append(jnp.concatenate(pieces, axis=1))
        span = pl.ds(pl.multiple_of(b * BLK, BLK), BLK)
        mine = direct[span, :] + dot(jnp.concatenate(normed, axis=0), mixed[...])
        for c in range(BLK // ROW):
            feats[2 * b + c] = mine[c * ROW:(c + 1) * ROW].astype(BF16)
        return carry

    lax.fori_loop(0, blocks, project, 0, unroll=4)

    cell_ids = lax.broadcasted_iota(jnp.int32, (CELLS, ROW), 0)

    def across(r):
        target = wide
        for s in range(bits):
            target = target + (r // 2**s) % 2 * 2**s * (1 - 2 * ((wide // 2**s) % 2))
        return target

    def partial_pool(brick):
        marks, sources = [], []
        for m in range(most):
            row = slots[brick * most + m]
            at = jnp.maximum(row, 0)
            cells = cell_ref[pl.ds(at, 1), :] + jnp.where(row < 0, -CELLS, 0)
            marks.append(jnp.where(cell_ids == cells, 1.0, 0.0).astype(BF16))
            sources.append(feats[at])
        return dot(jnp.concatenate(marks, axis=1), jnp.concatenate(sources, axis=0))

    def turned(label, k):
        return swap_bits(label) if k == SWAPPED else label

    def piece_copy(label, bit, k):
        span = pl.ds(k * PIECE, PIECE)
        return remote(
            part_send.at[label - 1, span], part_recv.at[label - 1, span],
            sa.at[label - 1, k], ra.at[label - 1, k], across(turned(bit, k)), narrow,
        )

    odd = range(wide_count - 1, 0, -2)
    even = range(wide_count - 2, -1, -2)
    for distance in [*odd, *even]:
        pool = partial_pool(across(distance))
        for k in PIECE_ORDER:
            label = turned(distance, k)
            span = slice(k * PIECE, (k + 1) * PIECE)
            if label % 2:
                part_send[label - 1, span] = pool[span].astype(BF16)
                piece_copy(label, 1, k).start()
            else:
                own_part[label // 2, span] = pool[span]

    def halo_copy(k, dy, dx):
        if dy == 0:
            source = pooled.at[:, pl.ds(BY - EDGE if dx > 0 else 0, EDGE)]
            target = cols_recv.at[0 if dx > 0 else 1]
        else:
            span = pl.ds(BX - HALO if dy > 0 else 0, HALO)
            if dx == 0:
                source = pooled.at[span]
                target = rows_recv.at[0 if dy > 0 else 1]
            else:
                source = pooled.at[span, pl.ds(BY - EDGE if dx > 0 else 0, EDGE)]
                target = corner_recv.at[(0 if dy > 0 else 2) + (0 if dx > 0 else 1)]
        return remote(
            source, target, sh.at[k], rh.at[k],
            (wide + dy + wide_count) % wide_count, (narrow + dx + narrow_count) % narrow_count,
        )

    steps = [(dy, dx) for dy in (-1, 1) for dx in (0, -1, 1)] + [(0, -1), (0, 1)]

    def inside(dy, dx):
        return (
            (wide + dy >= 0) & (wide + dy < wide_count)
            & (narrow + dx >= 0) & (narrow + dx < narrow_count)
        )

    def send_halo(wanted):
        for k, (dy, dx) in enumerate(steps):
            if dy != wanted:
                continue

            @pl.when(inside(dy, dx))
            def _(k=k, dy=dy, dx=dx):
                halo_copy(k, dy, dx).start()

    for label in even:
        low = label & -label if label else wide_count
        for k in PIECE_ORDER:
            span = slice(k * PIECE, (k + 1) * PIECE)
            summed = own_part[label // 2, span]
            bit = 1
            while bit < low:
                piece_copy(label + bit, bit, k).wait_recv()
                summed = summed + part_recv[label + bit - 1, span].astype(F32)
                bit *= 2
            if label:
                part_send[label - 1, span] = summed.astype(BF16)
                piece_copy(label, low, k).start()
            else:
                lines = slice(k * PIECE // BY, (k + 1) * PIECE // BY)
                done = summed.astype(BF16).reshape(PIECE // BY, BY, PF)
                pooled[lines] = done
                ext[HALO + lines.start:HALO + lines.stop, EDGE:EDGE + BY, :] = done
                if k == 0:
                    send_halo(-1)
                if k == PIECES - 1:
                    send_halo(1)
    send_halo(0)

    def take_halo(across_rows):
        for k, (dy, dx) in enumerate(steps):
            if (dy != 0) != across_rows:
                continue

            @pl.when(inside(-dy, -dx))
            def _(k=k, dy=dy, dx=dx):
                halo_copy(k, dy, dx).wait_recv()
                span = slice(HALO, HALO + BX)
                if dy > 0:
                    span = slice(0, HALO)
                elif dy < 0:
                    span = slice(HALO + BX, 2 * HALO + BX)
                if dx == 0:
                    ext[span, EDGE:EDGE + BY, :] = rows_recv[0 if dy > 0 else 1]
                else:
                    columns = slice(0, EDGE) if dx > 0 else slice(EDGE + BY, WIDTH)
                    if dy == 0:
                        ext[span, columns, :] = cols_recv[0 if dx > 0 else 1]
                    else:
                        ext[span, columns, :] = corner_recv[(0 if dy > 0 else 2) + (0 if dx > 0 else 1)]

    def convolve(field, weight, start, height):
        size = height * WIDTH
        result = None
        for dx in range(3):
            shifted = None
            for dy in range(3):
                window = field[start + dy:start + dy + height].reshape(size, PF)
                term = dot(window, weight[dy, dx])
                shifted = term if shifted is None else shifted + term
            if dx != 1:
                shifted = pltpu.roll(shifted, 1 if dx == 0 else size - 1, 0)
            result = shifted if result is None else result + shifted
        return result.reshape(height, WIDTH, PF)

    def first_layer(start, height):
        active = jax.nn.gelu(convolve(ext, first, start, height), approximate=True)
        extent = (height, WIDTH, PF)
        grid_row = lax.broadcasted_iota(jnp.int32, extent, 0) + wide * BX + start - 1
        grid_column = lax.broadcasted_iota(jnp.int32, extent, 1) + narrow * BY - EDGE
        real = (
            (grid_row >= 0) & (grid_row < wide_count * BX)
            & (grid_column >= 0) & (grid_column < narrow_count * BY)
        )
        inner[start:start + height] = jnp.where(real, active, 0.0).astype(BF16)

    def second_layer(start, height):
        out_ref[start:start + height] = convolve(inner, second, start, height)[:, EDGE:EDGE + BY, :]

    loads[3].wait()
    loads[4].wait()
    take_halo(False)
    first_layer(HALO, BX - HALO)
    second_layer(HALO, BX - 2 * HALO)
    take_halo(True)
    first_layer(0, HALO)
    first_layer(BX, HALO)
    second_layer(0, HALO)
    second_layer(BX - HALO, HALO)

    for j in range(PARTS):
        for t in range(1, members):
            gather_copy(t, j).wait_send()
            spread_copy(t, j).wait_send()
        for t in range(1, quads):
            @pl.when(quad + t < quads)
            def _(t=t, j=j):
                later_copy(t, j).wait_send()

    for label in range(1, wide_count):
        for k in range(PIECES):
            piece_copy(label, label & -label, k).wait_send()
    for k, (dy, dx) in enumerate(steps):
        @pl.when(inside(dy, dx))
        def _(k=k, dy=dy, dx=dx):
            halo_copy(k, dy, dx).wait_send()


def per_device(voxels, w_qkv, w_out, w_feature, conv_first, conv_second, row_brick, cell_place):
    token_count = voxels.shape[0]
    rows = token_count // ROW
    wide_count = lax.axis_size("wide")
    narrow_count = lax.axis_size("narrow")
    blocks = token_count // BLK
    quads = wide_count // 2
    members = 2 * narrow_count
    others = max(1, quads - 1)
    most = 2 * (-(-rows // wide_count))
    anywhere = pl.BlockSpec(memory_space=pl.ANY)
    vmem = pl.BlockSpec(memory_space=pltpu.VMEM)
    smem = pl.BlockSpec(memory_space=pltpu.SMEM)
    dma = pltpu.SemaphoreType.DMA
    state = (HEAD, HEAD)
    grid = (CELLS, PF)
    scratch = [
        pltpu.VMEM(voxels.shape, BF16),
        pltpu.VMEM(w_qkv.shape, BF16),
        pltpu.VMEM(w_out.shape, BF16),
        pltpu.VMEM(w_feature.shape, BF16),
        pltpu.VMEM(conv_first.shape, BF16),
        pltpu.VMEM(conv_second.shape, BF16),
        pltpu.VMEM((token_count, 2 * D), BF16),
        pltpu.VMEM((token_count, D), BF16),
        pltpu.VMEM((token_count, D), F32),
        pltpu.VMEM((token_count, PF), F32),
        pltpu.VMEM((D, PF), BF16),
        pltpu.VMEM((rows, HEADS) + state, BF16),
        pltpu.VMEM((HEADS,) + state, F32),
        pltpu.VMEM((rows, ROW, PF), BF16),
        pltpu.SMEM((wide_count * most,), jnp.int32),
        pltpu.VMEM((members,) + state, BF16),
        pltpu.VMEM((members,) + state, BF16),
        pltpu.VMEM(state, BF16),
        pltpu.VMEM((others,) + state, BF16),
        pltpu.VMEM((members,) + state, BF16),
        pltpu.VMEM((members,) + state, BF16),
        pltpu.VMEM((wide_count - 1,) + grid, BF16),
        pltpu.VMEM((wide_count - 1,) + grid, BF16),
        pltpu.VMEM((quads,) + grid, F32),
        pltpu.VMEM((BX, BY, PF), BF16),
        pltpu.VMEM((BX + 2 * HALO, WIDTH, PF), BF16),
        pltpu.VMEM((2, HALO, BY, PF), BF16),
        pltpu.VMEM((2, BX, EDGE, PF), BF16),
        pltpu.VMEM((4, HALO, EDGE, PF), BF16),
        pltpu.VMEM((BX + 2, WIDTH, PF), BF16),
        dma((blocks,)),
        dma((6,)),
        dma((members - 1, PARTS)), dma((members - 1, PARTS)),
        dma((others, PARTS)), dma((others, PARTS)),
        dma((members - 1, PARTS)), dma((members - 1, PARTS)),
        dma((wide_count - 1, PIECES)), dma((wide_count - 1, PIECES)),
        dma((8,)), dma((8,)),
    ]
    return pl.pallas_call(
        functools.partial(kernel, wide_count, narrow_count, token_count, most),
        out_shape=jax.ShapeDtypeStruct((BX, BY, PF), F32),
        in_specs=[anywhere] * 6 + [smem, vmem],
        out_specs=vmem,
        scratch_shapes=scratch,
        compiler_params=pltpu.CompilerParams(
            collective_id=0, has_side_effects=True, vmem_limit_bytes=56 * 1024 * 1024
        ),
        name="scene_flow",
    )(
        voxels, w_qkv, w_out, w_feature, conv_first, conv_second,
        row_brick.reshape(1, rows), cell_place.reshape(rows, ROW),
    )


def solution(mesh):
    placed = (
        P(("group", "wide", "narrow"), None),
        P(),
        P(),
        P(),
        P(),
        P(),
        P(("group", "wide", "narrow"), None),
        P(("group", "wide", "narrow")),
    )
    return jax.shard_map(
        per_device,
        mesh=mesh,
        in_specs=placed,
        out_specs=P(("group", "wide"), "narrow", None),
        check_vma=False,
    )
```

```python
import functools
import math

import jax
import jax.numpy as jnp
from jax import lax
from jax.experimental import pallas as pl
from jax.experimental.pallas import tpu as pltpu
from jax.sharding import PartitionSpec as P

D = 512
HEADS = 4
HEAD = 128
PF = 256
ROW = 128
BLK = 256
PER = BLK // ROW
BX = 8
BY = 32
CELLS = BX * BY
PAIR = 2 * HEAD
EDGE = 16
MIDDLE = D // 2
WIDTH = BY + 2 * EDGE
HALO = 2
PIECES = 4
PIECE = CELLS // PIECES
PIECE_ORDER = (0, 3, 1, 2)
PARTS = 2
PART = HEAD // PARTS

epsilon = 1e-06
MESH = pl.DeviceIdType.MESH
F32 = jnp.float32
BF16 = jnp.bfloat16


def dot(a, b):
    return jnp.dot(a, b, preferred_element_type=F32)


def dot_t(a, b):
    return lax.dot_general(a, b, (((0,), (0,)), ((), ())), preferred_element_type=F32)


def dot_nt(a, b):
    return lax.dot_general(a, b, (((1,), (1,)), ((), ())), preferred_element_type=F32)


def diagonal(upper, lower):
    blank_right = jnp.zeros((upper.shape[0], lower.shape[1]), upper.dtype)
    blank_left = jnp.zeros((lower.shape[0], upper.shape[1]), lower.dtype)
    return jnp.concatenate(
        [
            jnp.concatenate([upper, blank_right], axis=1),
            jnp.concatenate([blank_left, lower], axis=1),
        ],
        axis=0,
    )


def kernel(
    wide_count, narrow_count, token_count, most,
    vox_hbm, wqkv_hbm, wout_hbm, wfeat_hbm, first_hbm, second_hbm, brick_ref, cell_ref,
    out_ref,
    vox, wqkv, wout, wfeat, first, second,
    kv, qs, att, direct, mixed, within, total, feats, slots, gram_upper, gram_lower, seen, base,
    own_total, quad_parts, quad_send, quad_recv, prefix_send, prefix_recv,
    part_send, part_recv, own_part,
    pooled, ext, rows_recv, cols_recv, corner_recv, inner,
    vox_sem, load_sem,
    s1, r1, s2, r2, s3, r3, sa, ra, sh, rh,
):
    blocks = token_count // BLK
    rows = token_count // ROW
    quads = wide_count // 2
    bits = wide_count.bit_length() - 1
    wide = lax.axis_index("wide")
    narrow = lax.axis_index("narrow")
    side = wide % 2
    quad = wide // 2
    members = 2 * narrow_count
    place = side * narrow_count + narrow

    def load_vox(b):
        span = pl.ds(pl.multiple_of(b * BLK, BLK), BLK)
        return pltpu.make_async_copy(vox_hbm.at[span], vox.at[span], vox_sem.at[b])

    def load(source, target, k):
        return pltpu.make_async_copy(source, target, load_sem.at[k])

    loads = [
        load(wqkv_hbm.at[:, pl.ds(D, 2 * D)], wqkv.at[:, pl.ds(D, 2 * D)], 0),
        load(wout_hbm, wout, 1),
        load(wfeat_hbm, wfeat, 2),
        load(first_hbm, first, 3),
        load(second_hbm, second, 4),
        load(wqkv_hbm.at[:, pl.ds(0, D)], wqkv.at[:, pl.ds(0, D)], 5),
    ]
    for b in range(blocks):
        load_vox(b).start()
    for k in (0, 5, 2, 1, 3, 4):
        loads[k].start()

    barrier = pltpu.get_barrier_semaphore()
    beside = (wide + wide_count + 2 * side - 1) % wide_count
    partners = [
        (quad * 2 + (place + t) % members // narrow_count, (place + t) % narrow_count)
        for t in range(1, members)
    ]
    partners += [((quad + t) % quads * 2 + side, narrow) for t in range(1, quads)]
    partners += [(beside, n) for n in range(narrow_count)]
    for to_wide, to_narrow in partners:
        pl.semaphore_signal(
            barrier, inc=1, device_id={"wide": to_wide, "narrow": to_narrow}, device_id_type=MESH
        )

    def remote(source, target, send_sem, recv_sem, to_wide, to_narrow):
        return pltpu.make_async_remote_copy(
            src_ref=source, dst_ref=target, send_sem=send_sem, recv_sem=recv_sem,
            device_id={"wide": to_wide, "narrow": to_narrow}, device_id_type=MESH,
        )

    causal = lax.broadcasted_iota(jnp.int32, (ROW, PAIR), 0) >= (
        lax.broadcasted_iota(jnp.int32, (ROW, PAIR), 1) % ROW
    )
    total[...] = jnp.zeros_like(total)
    ext[...] = jnp.zeros_like(ext)

    def gram(start, stop):
        span = slice(start, stop)
        upper = dot_t(vox[span, :MIDDLE], vox[span, :])
        lower = dot_t(vox[span, MIDDLE:], vox[span, MIDDLE:])
        return upper, lower

    half = token_count // 2
    for b in range(blocks // 2):
        load_vox(b).wait()
    gram_upper[...], gram_lower[...] = gram(0, half)
    for b in range(blocks // 2, blocks):
        load_vox(b).wait()
    upper, lower = gram(half, token_count)
    upper = (gram_upper[...] + upper).astype(BF16)
    lower = (gram_lower[...] + lower).astype(BF16)
    loads[0].wait()
    seen[:MIDDLE] = dot(upper, wqkv[:, 2 * D:]).astype(BF16)
    seen[MIDDLE:] = (
        dot_t(upper[:, MIDDLE:], wqkv[:MIDDLE, 2 * D:]) + dot(lower, wqkv[MIDDLE:, 2 * D:])
    ).astype(BF16)
    for p in range(HEADS // 2):
        columns = slice(p * PAIR, (p + 1) * PAIR)
        state = dot_t(wqkv[:, D + p * PAIR:D + (p + 1) * PAIR], seen[:, columns])
        for i in range(2):
            corner = slice(i * HEAD, (i + 1) * HEAD)
            own_total[2 * p + i] = state[corner, corner].astype(BF16)
    pl.semaphore_wait(barrier, len(partners))

    def part_rows(j):
        return pl.ds(j * PART, PART)

    def member(t):
        other = (place + t) % members
        return other, quad * 2 + other // narrow_count, other % narrow_count

    def gather_copy(t, j):
        other, to_wide, to_narrow = member(t)
        return remote(
            own_total.at[other, part_rows(j)], quad_parts.at[t - 1, part_rows(j)],
            s1.at[t - 1, j], r1.at[t - 1, j], to_wide, to_narrow,
        )

    for j in range(PARTS):
        for t in range(1, members):
            gather_copy(t, j).start()

    def inputs(b):
        span = slice(b * BLK, (b + 1) * BLK)
        if b == 0:
            loads[5].wait()
            loads[2].wait()
        kv[span, :] = dot(vox[span, :], wqkv[:, D:]).astype(BF16)
        query = dot(vox[span, :], wqkv[:, :D]).astype(BF16)
        qs[PER * b:PER * (b + 1)] = query.reshape(PER, ROW, D)
        direct[PER * b:PER * (b + 1)] = dot(vox[span, :], wfeat[...]).reshape(PER, ROW, PF)

    def local(b):
        for h in range(HEADS):
            mine = slice(h * HEAD, (h + 1) * HEAD)
            other = slice(D + h * HEAD, D + (h + 1) * HEAD)
            first_chunk = slice(b * BLK, b * BLK + ROW)
            second_chunk = slice(b * BLK + ROW, (b + 1) * BLK)
            state = dot_t(
                kv[b * BLK:(b + 1) * BLK, mine], diagonal(kv[first_chunk, other], kv[second_chunk, other])
            )
            before = total[h]
            within[2 * b, h] = before.astype(BF16)
            middle = before + state[:, :HEAD]
            within[2 * b + 1, h] = middle.astype(BF16)
            total[h] = middle + state[:, HEAD:]
        scores = {}
        for c in range(PER):
            row = b * PER + c
            chunk = slice(row * ROW, (row + 1) * ROW)
            for p in range(HEADS // 2):
                low, high = 2 * p * HEAD, (2 * p + 1) * HEAD
                keys = diagonal(kv[chunk, low:low + HEAD], kv[chunk, high:high + HEAD])
                both = dot_nt(qs[row, :, p * PAIR:(p + 1) * PAIR], keys)
                scores[c, p] = jnp.where(causal, both, 0.0).astype(BF16)
        for c in range(PER):
            row = b * PER + c
            chunk = slice(row * ROW, (row + 1) * ROW)
            for p in range(HEADS // 2):
                low, high = D + 2 * p * HEAD, D + (2 * p + 1) * HEAD
                values = diagonal(kv[chunk, low:low + HEAD], kv[chunk, high:high + HEAD])
                att[row, :, p * PAIR:(p + 1) * PAIR] = dot(scores[c, p], values)

    def within_device(start, stop):
        for b in range(start, stop):
            if b < blocks:
                inputs(b)
            if b > 0:
                local(b - 1)

    cut_one = blocks // 2
    cut_two = blocks
    within_device(0, cut_one)

    def later_copy(t, j):
        return remote(
            quad_send.at[part_rows(j)], quad_recv.at[t - 1, part_rows(j)],
            s2.at[t - 1, j], r2.at[t - 1, j],
            ((quad + t) % quads) * 2 + side, narrow,
        )

    for j in range(PARTS):
        piece = slice(j * PART, (j + 1) * PART)
        for t in range(1, members):
            gather_copy(t, j).wait_recv()
        quad_sum = own_total[place, piece].astype(F32)
        for t in range(1, members):
            quad_sum = quad_sum + quad_parts[t - 1, piece].astype(F32)
        quad_send[piece] = quad_sum.astype(BF16)
        for t in range(1, quads):
            @pl.when(quad + t < quads)
            def _(t=t, j=j):
                later_copy(t, j).start()

    within_device(cut_one, cut_two)
    loads[1].wait()
    mixed[...] = dot(wout[...], wfeat[...]).astype(BF16)

    def assign(b, carry):
        held = [jnp.int32(-1)] * most
        for r in range(rows):
            hit = brick_ref[0, r] == b
            held = [
                jnp.where(hit, jnp.int32(r) if m == 0 else held[m - 1], held[m]) for m in range(most)
            ]
        for m in range(most):
            slots[b * most + m] = held[m]
        return carry

    lax.fori_loop(0, wide_count, assign, 0)

    def spread_copy(t, j):
        other, to_wide, to_narrow = member(t)
        return remote(
            prefix_send.at[other, part_rows(j)], prefix_recv.at[place, part_rows(j)],
            s3.at[t - 1, j], r3.at[t - 1, j], to_wide, to_narrow,
        )

    def spread_arrival(t, j):
        source = (place - t + members) % members
        return remote(
            prefix_send.at[source, part_rows(j)], prefix_recv.at[source, part_rows(j)],
            s3.at[t - 1, j], r3.at[t - 1, j], wide, narrow,
        )

    for j in range(PARTS):
        piece = slice(j * PART, (j + 1) * PART)
        base[piece] = jnp.zeros((PART, HEAD), F32)
        for t in range(1, quads):
            @pl.when(quad - t >= 0)
            def _(t=t, j=j, piece=piece):
                later_copy(t, j).wait_recv()
                base[piece] = base[piece] + quad_recv[t - 1, piece].astype(F32)
        running = base[piece]
        for m in range(members):
            prefix_send[m, piece] = running.astype(BF16)
            if m < members - 1:
                value = own_total[place, piece].astype(F32)
                for t in range(1, members):
                    value = jnp.where(
                        (place - t + members) % members == m,
                        quad_parts[t - 1, piece].astype(F32), value,
                    )
                running = running + value
        for t in range(1, members):
            spread_copy(t, j).start()
        prefix_recv[place, piece] = prefix_send[place, piece]

    within_device(cut_two, blocks + 1)

    for j in range(PARTS):
        for t in range(1, members):
            spread_arrival(t, j).wait_recv()
    for h in range(HEADS):
        total[h] = prefix_recv[h].astype(F32)

    def state_of(row, p):
        return diagonal(*[
            (within[row, 2 * p + i].astype(F32) + total[2 * p + i]).astype(BF16) for i in range(2)
        ])

    def scaled(one):
        square = jnp.mean(one * one, axis=-1, keepdims=True)
        return (one * lax.rsqrt(square + epsilon)).astype(BF16)

    def attend(b):
        for row in range(PER * b, PER * (b + 1)):
            for p in range(HEADS // 2):
                columns = slice(p * PAIR, (p + 1) * PAIR)
                att[row, :, columns] += dot(qs[row, :, columns], state_of(row, p))

    def normalise(b):
        for row in range(PER * b, PER * (b + 1)):
            for h in range(HEADS):
                mine = slice(h * HEAD, (h + 1) * HEAD)
                qs[row, :, mine] = scaled(att[row, :, mine])

    def finish(b):
        span = slice(PER * b, PER * (b + 1))
        normed = qs[span].reshape(BLK, D)
        mine = direct[span].reshape(BLK, PF) + dot(normed, mixed[...])
        feats[span] = mine.astype(BF16).reshape(PER, ROW, PF)

    def project():
        for b in range(blocks + 2):
            if b < blocks:
                attend(b)
            if 0 < b <= blocks:
                normalise(b - 1)
            if b > 1:
                finish(b - 2)

    cell_ids = lax.broadcasted_iota(jnp.int32, (CELLS, ROW), 0)

    def across(r):
        target = wide
        for s in range(bits):
            target = target + (r // 2**s) % 2 * 2**s * (1 - 2 * ((wide // 2**s) % 2))
        return target

    def named_rows(brick):
        marks, chosen = [], []
        for m in range(most):
            named = slots[brick * most + m]
            row = jnp.maximum(named, 0)
            cells = cell_ref[pl.ds(row, 1), :] + jnp.where(named < 0, -CELLS, 0)
            marks.append(jnp.where(cell_ids == cells, 1.0, 0.0).astype(BF16))
            chosen.append(row)
        return jnp.concatenate(marks, axis=1), chosen

    def pool_ready(brick):
        marks, chosen = named_rows(brick)
        return dot(marks, jnp.concatenate([feats[row] for row in chosen], axis=0))

    def pool_afresh(brick):
        marks, chosen = named_rows(brick)
        normed, plain = [], []
        for row in chosen:
            pieces = []
            for p in range(HEADS // 2):
                columns = slice(p * PAIR, (p + 1) * PAIR)
                attended = att[row, :, columns] + dot(qs[row, :, columns], state_of(row, p))
                pieces += [scaled(attended[:, i * HEAD:(i + 1) * HEAD]) for i in range(2)]
            normed.append(jnp.concatenate(pieces, axis=1))
            plain.append(direct[row])
        features = jnp.concatenate(plain, axis=0) + dot(jnp.concatenate(normed, axis=0), mixed[...])
        return dot(marks, features.astype(BF16))

    def piece_copy(label, bit, k):
        span = pl.ds(k * PIECE, PIECE)
        return remote(
            part_send.at[label - 1, span], part_recv.at[label - 1, span],
            sa.at[label - 1, k], ra.at[label - 1, k], across(bit), narrow,
        )

    def send_partner(label, pool):
        part_send[label - 1] = pool.astype(BF16)
        for k in PIECE_ORDER:
            piece_copy(label, 1, k).start()

    send_partner(wide_count - 1, pool_afresh(across(wide_count - 1)))
    project()
    for label in range(wide_count - 3, 0, -2):
        send_partner(label, pool_ready(across(label)))
    for label in range(wide_count - 2, -1, -2):
        own_part[label // 2] = pool_ready(across(label))

    def halo_copy(k, dy, dx):
        if dy == 0:
            source = pooled.at[:, pl.ds(BY - EDGE if dx > 0 else 0, EDGE)]
            target = cols_recv.at[0 if dx > 0 else 1]
        else:
            span = pl.ds(BX - HALO if dy > 0 else 0, HALO)
            if dx == 0:
                source = pooled.at[span]
                target = rows_recv.at[0 if dy > 0 else 1]
            else:
                source = pooled.at[span, pl.ds(BY - EDGE if dx > 0 else 0, EDGE)]
                target = corner_recv.at[(0 if dy > 0 else 2) + (0 if dx > 0 else 1)]
        return remote(
            source, target, sh.at[k], rh.at[k],
            (wide + dy + wide_count) % wide_count, (narrow + dx + narrow_count) % narrow_count,
        )

    steps = [(dy, dx) for dy in (-1, 1) for dx in (0, -1, 1)] + [(0, -1), (0, 1)]

    def inside(dy, dx):
        return (
            (wide + dy >= 0) & (wide + dy < wide_count)
            & (narrow + dx >= 0) & (narrow + dx < narrow_count)
        )

    def send_halo(wanted):
        for k, (dy, dx) in enumerate(steps):
            if dy != wanted:
                continue

            @pl.when(inside(dy, dx))
            def _(k=k, dy=dy, dx=dx):
                halo_copy(k, dy, dx).start()

    for label in range(wide_count - 2, -1, -2):
        low = label & -label if label else wide_count
        for k in PIECE_ORDER:
            span = slice(k * PIECE, (k + 1) * PIECE)
            summed = own_part[label // 2, span]
            bit = 1
            while bit < low:
                piece_copy(label + bit, bit, k).wait_recv()
                summed = summed + part_recv[label + bit - 1, span].astype(F32)
                bit *= 2
            if label:
                part_send[label - 1, span] = summed.astype(BF16)
                piece_copy(label, low, k).start()
            else:
                lines = slice(k * PIECE // BY, (k + 1) * PIECE // BY)
                done = summed.astype(BF16).reshape(PIECE // BY, BY, PF)
                pooled[lines] = done
                ext[HALO + lines.start:HALO + lines.stop, EDGE:EDGE + BY, :] = done
                if k == 0:
                    send_halo(-1)
                if k == PIECES - 1:
                    send_halo(1)
    send_halo(0)

    def take_halo(across_rows):
        for k, (dy, dx) in enumerate(steps):
            if (dy != 0) != across_rows:
                continue

            @pl.when(inside(-dy, -dx))
            def _(k=k, dy=dy, dx=dx):
                halo_copy(k, dy, dx).wait_recv()
                span = slice(HALO, HALO + BX)
                if dy > 0:
                    span = slice(0, HALO)
                elif dy < 0:
                    span = slice(HALO + BX, 2 * HALO + BX)
                if dx == 0:
                    ext[span, EDGE:EDGE + BY, :] = rows_recv[0 if dy > 0 else 1]
                else:
                    columns = slice(0, EDGE) if dx > 0 else slice(EDGE + BY, WIDTH)
                    if dy == 0:
                        ext[span, columns, :] = cols_recv[0 if dx > 0 else 1]
                    else:
                        ext[span, columns, :] = corner_recv[(0 if dy > 0 else 2) + (0 if dx > 0 else 1)]

    def convolve(field, weight, start, height):
        size = height * WIDTH
        result = None
        for dx in range(3):
            shifted = None
            for dy in range(3):
                window = field[start + dy:start + dy + height].reshape(size, PF)
                term = dot(window, weight[dy, dx])
                shifted = term if shifted is None else shifted + term
            if dx != 1:
                shifted = pltpu.roll(shifted, 1 if dx == 0 else size - 1, 0)
            result = shifted if result is None else result + shifted
        return result.reshape(height, WIDTH, PF)

    def first_layer(start, height):
        active = jax.nn.gelu(convolve(ext, first, start, height), approximate=True)
        extent = (height, WIDTH, PF)
        grid_row = lax.broadcasted_iota(jnp.int32, extent, 0) + wide * BX + start - 1
        grid_column = lax.broadcasted_iota(jnp.int32, extent, 1) + narrow * BY - EDGE
        real = (
            (grid_row >= 0) & (grid_row < wide_count * BX)
            & (grid_column >= 0) & (grid_column < narrow_count * BY)
        )
        inner[start:start + height] = jnp.where(real, active, 0.0).astype(BF16)

    def second_layer(start, height):
        out_ref[start:start + height] = convolve(inner, second, start, height)[:, EDGE:EDGE + BY, :]

    loads[3].wait()
    loads[4].wait()
    take_halo(False)
    first_layer(HALO, BX - HALO)
    second_layer(HALO, BX - 2 * HALO)
    take_halo(True)
    first_layer(0, HALO)
    first_layer(BX, HALO)
    second_layer(0, HALO)
    second_layer(BX - HALO, HALO)

    for j in range(PARTS):
        for t in range(1, members):
            gather_copy(t, j).wait_send()
            spread_copy(t, j).wait_send()
        for t in range(1, quads):
            @pl.when(quad + t < quads)
            def _(t=t, j=j):
                later_copy(t, j).wait_send()

    for label in range(1, wide_count):
        for k in range(PIECES):
            piece_copy(label, label & -label, k).wait_send()
    for k, (dy, dx) in enumerate(steps):
        @pl.when(inside(dy, dx))
        def _(k=k, dy=dy, dx=dx):
            halo_copy(k, dy, dx).wait_send()


def per_device(voxels, w_qkv, w_out, w_feature, conv_first, conv_second, row_brick, cell_place):
    token_count = voxels.shape[0]
    rows = token_count // ROW
    wide_count = lax.axis_size("wide")
    narrow_count = lax.axis_size("narrow")
    blocks = token_count // BLK
    quads = wide_count // 2
    members = 2 * narrow_count
    others = max(1, quads - 1)
    most = 2 * (-(-rows // wide_count))
    anywhere = pl.BlockSpec(memory_space=pl.ANY)
    vmem = pl.BlockSpec(memory_space=pltpu.VMEM)
    smem = pl.BlockSpec(memory_space=pltpu.SMEM)
    dma = pltpu.SemaphoreType.DMA
    state = (HEAD, HEAD)
    grid = (CELLS, PF)
    scratch = [
        pltpu.VMEM(voxels.shape, BF16),
        pltpu.VMEM(w_qkv.shape, BF16),
        pltpu.VMEM(w_out.shape, BF16),
        pltpu.VMEM(w_feature.shape, BF16),
        pltpu.VMEM(conv_first.shape, BF16),
        pltpu.VMEM(conv_second.shape, BF16),
        pltpu.VMEM((token_count, 2 * D), BF16),
        pltpu.VMEM((rows, ROW, D), BF16),
        pltpu.VMEM((rows, ROW, D), F32),
        pltpu.VMEM((rows, ROW, PF), F32),
        pltpu.VMEM((D, PF), BF16),
        pltpu.VMEM((rows, HEADS) + state, BF16),
        pltpu.VMEM((HEADS,) + state, F32),
        pltpu.VMEM((rows, ROW, PF), BF16),
        pltpu.SMEM((wide_count * most,), jnp.int32),
        pltpu.VMEM((MIDDLE, D), F32),
        pltpu.VMEM((MIDDLE, MIDDLE), F32),
        pltpu.VMEM((D, D), BF16),
        pltpu.VMEM(state, F32),
        pltpu.VMEM((members,) + state, BF16),
        pltpu.VMEM((members,) + state, BF16),
        pltpu.VMEM(state, BF16),
        pltpu.VMEM((others,) + state, BF16),
        pltpu.VMEM((members,) + state, BF16),
        pltpu.VMEM((members,) + state, BF16),
        pltpu.VMEM((wide_count - 1,) + grid, BF16),
        pltpu.VMEM((wide_count - 1,) + grid, BF16),
        pltpu.VMEM((quads,) + grid, F32),
        pltpu.VMEM((BX, BY, PF), BF16),
        pltpu.VMEM((BX + 2 * HALO, WIDTH, PF), BF16),
        pltpu.VMEM((2, HALO, BY, PF), BF16),
        pltpu.VMEM((2, BX, EDGE, PF), BF16),
        pltpu.VMEM((4, HALO, EDGE, PF), BF16),
        pltpu.VMEM((BX + 2, WIDTH, PF), BF16),
        dma((blocks,)),
        dma((6,)),
        dma((members - 1, PARTS)), dma((members - 1, PARTS)),
        dma((others, PARTS)), dma((others, PARTS)),
        dma((members - 1, PARTS)), dma((members - 1, PARTS)),
        dma((wide_count - 1, PIECES)), dma((wide_count - 1, PIECES)),
        dma((8,)), dma((8,)),
    ]
    return pl.pallas_call(
        functools.partial(kernel, wide_count, narrow_count, token_count, most),
        out_shape=jax.ShapeDtypeStruct((BX, BY, PF), F32),
        in_specs=[anywhere] * 6 + [smem, vmem],
        out_specs=vmem,
        scratch_shapes=scratch,
        compiler_params=pltpu.CompilerParams(
            collective_id=0, has_side_effects=True, vmem_limit_bytes=56 * 1024 * 1024
        ),
        name="scene_flow",
    )(
        voxels, w_qkv, w_out, w_feature, conv_first, conv_second,
        row_brick.reshape(1, rows), cell_place.reshape(rows, ROW),
    )


def solution(mesh):
    placed = (
        P(("group", "wide", "narrow"), None),
        P(),
        P(),
        P(),
        P(),
        P(),
        P(("group", "wide", "narrow"), None),
        P(("group", "wide", "narrow")),
    )
    return jax.shard_map(
        per_device,
        mesh=mesh,
        in_specs=placed,
        out_specs=P(("group", "wide"), "narrow", None),
        check_vma=False,
    )
```

```python
import functools
import math

import jax
import jax.numpy as jnp
from jax import lax
from jax.experimental import pallas as pl
from jax.experimental.pallas import tpu as pltpu
from jax.sharding import PartitionSpec as P

D = 512
HEADS = 4
HEAD = 128
PF = 256
ROW = 128
BLK = 256
PER = BLK // ROW
BX = 8
BY = 32
CELLS = BX * BY
PAIR = 2 * HEAD
EDGE = 16
MIDDLE = D // 2
WIDTH = BY + 2 * EDGE
HALO = 2
PIECES = 4
PIECE = CELLS // PIECES
PIECE_ORDER = (0, 3, 1, 2)
PARTS = 2
PART = HEAD // PARTS

epsilon = 1e-06
MESH = pl.DeviceIdType.MESH
F32 = jnp.float32
BF16 = jnp.bfloat16


def dot(a, b):
    return jnp.dot(a, b, preferred_element_type=F32)


def dot_t(a, b):
    return lax.dot_general(a, b, (((0,), (0,)), ((), ())), preferred_element_type=F32)


def dot_nt(a, b):
    return lax.dot_general(a, b, (((1,), (1,)), ((), ())), preferred_element_type=F32)


def diagonal(upper, lower):
    blank_right = jnp.zeros((upper.shape[0], lower.shape[1]), upper.dtype)
    blank_left = jnp.zeros((lower.shape[0], upper.shape[1]), lower.dtype)
    return jnp.concatenate(
        [
            jnp.concatenate([upper, blank_right], axis=1),
            jnp.concatenate([blank_left, lower], axis=1),
        ],
        axis=0,
    )


def kernel(
    wide_count, narrow_count, token_count, most,
    vox_hbm, wqkv_hbm, wout_hbm, wfeat_hbm, first_hbm, second_hbm, brick_ref, cell_ref,
    out_ref,
    vox, wqkv, wout, wfeat, first, second,
    kv, qs, att, direct, mixed, within, total, feats, slots, gram_upper, gram_lower, seen, base,
    own_total, quad_parts, quad_send, quad_recv, prefix_send, prefix_recv,
    part_send, part_recv, own_part,
    pooled, ext, rows_recv, cols_recv, corner_recv, inner,
    vox_sem, load_sem,
    s1, r1, s2, r2, s3, r3, sa, ra, sh, rh,
):
    blocks = token_count // BLK
    rows = token_count // ROW
    quads = wide_count // 2
    bits = wide_count.bit_length() - 1
    wide = lax.axis_index("wide")
    narrow = lax.axis_index("narrow")
    side = wide % 2
    quad = wide // 2
    members = 2 * narrow_count
    place = side * narrow_count + narrow

    def load_vox(b):
        span = pl.ds(pl.multiple_of(b * BLK, BLK), BLK)
        return pltpu.make_async_copy(vox_hbm.at[span], vox.at[span], vox_sem.at[b])

    def load(source, target, k):
        return pltpu.make_async_copy(source, target, load_sem.at[k])

    loads = [
        load(wqkv_hbm.at[:, pl.ds(D, 2 * D)], wqkv.at[:, pl.ds(D, 2 * D)], 0),
        load(wout_hbm, wout, 1),
        load(wfeat_hbm, wfeat, 2),
        load(first_hbm, first, 3),
        load(second_hbm, second, 4),
        load(wqkv_hbm.at[:, pl.ds(0, D)], wqkv.at[:, pl.ds(0, D)], 5),
    ]
    for b in range(blocks):
        load_vox(b).start()
    for k in (0, 5, 2, 1, 3, 4):
        loads[k].start()

    barrier = pltpu.get_barrier_semaphore()
    beside = (wide + wide_count + 2 * side - 1) % wide_count
    partners = [
        (quad * 2 + (place + t) % members // narrow_count, (place + t) % narrow_count)
        for t in range(1, members)
    ]
    partners += [((quad + t) % quads * 2 + side, narrow) for t in range(1, quads)]
    partners += [(beside, n) for n in range(narrow_count)]
    for to_wide, to_narrow in partners:
        pl.semaphore_signal(
            barrier, inc=1, device_id={"wide": to_wide, "narrow": to_narrow}, device_id_type=MESH
        )

    def remote(source, target, send_sem, recv_sem, to_wide, to_narrow):
        return pltpu.make_async_remote_copy(
            src_ref=source, dst_ref=target, send_sem=send_sem, recv_sem=recv_sem,
            device_id={"wide": to_wide, "narrow": to_narrow}, device_id_type=MESH,
        )

    causal = lax.broadcasted_iota(jnp.int32, (ROW, PAIR), 0) >= (
        lax.broadcasted_iota(jnp.int32, (ROW, PAIR), 1) % ROW
    )
    total[...] = jnp.zeros_like(total)
    ext[...] = jnp.zeros_like(ext)

    def gram(start, stop):
        span = slice(start, stop)
        upper = dot_t(vox[span, :MIDDLE], vox[span, :])
        lower = dot_t(vox[span, MIDDLE:], vox[span, MIDDLE:])
        return upper, lower

    half = token_count // 2
    for b in range(blocks // 2):
        load_vox(b).wait()
    gram_upper[...], gram_lower[...] = gram(0, half)
    for b in range(blocks // 2, blocks):
        load_vox(b).wait()
    upper, lower = gram(half, token_count)
    upper = (gram_upper[...] + upper).astype(BF16)
    lower = (gram_lower[...] + lower).astype(BF16)
    loads[0].wait()
    seen[:MIDDLE] = dot(upper, wqkv[:, 2 * D:]).astype(BF16)
    seen[MIDDLE:] = (
        dot_t(upper[:, MIDDLE:], wqkv[:MIDDLE, 2 * D:]) + dot(lower, wqkv[MIDDLE:, 2 * D:])
    ).astype(BF16)
    for p in range(HEADS // 2):
        columns = slice(p * PAIR, (p + 1) * PAIR)
        state = dot_t(wqkv[:, D + p * PAIR:D + (p + 1) * PAIR], seen[:, columns])
        for i in range(2):
            corner = slice(i * HEAD, (i + 1) * HEAD)
            own_total[2 * p + i] = state[corner, corner].astype(BF16)
    pl.semaphore_wait(barrier, len(partners))

    def part_rows(j):
        return pl.ds(j * PART, PART)

    def member(t):
        other = (place + t) % members
        return other, quad * 2 + other // narrow_count, other % narrow_count

    def gather_copy(t, j):
        other, to_wide, to_narrow = member(t)
        return remote(
            own_total.at[other, part_rows(j)], quad_parts.at[t - 1, part_rows(j)],
            s1.at[t - 1, j], r1.at[t - 1, j], to_wide, to_narrow,
        )

    for j in range(PARTS):
        for t in range(1, members):
            gather_copy(t, j).start()

    def inputs(b):
        span = slice(b * BLK, (b + 1) * BLK)
        if b == 0:
            loads[5].wait()
            loads[2].wait()
        kv[span, :] = dot(vox[span, :], wqkv[:, D:]).astype(BF16)
        query = dot(vox[span, :], wqkv[:, :D]).astype(BF16)
        qs[PER * b:PER * (b + 1)] = query.reshape(PER, ROW, D)
        direct[PER * b:PER * (b + 1)] = dot(vox[span, :], wfeat[...]).reshape(PER, ROW, PF)

    def local(b):
        for h in range(HEADS):
            mine = slice(h * HEAD, (h + 1) * HEAD)
            other = slice(D + h * HEAD, D + (h + 1) * HEAD)
            first_chunk = slice(b * BLK, b * BLK + ROW)
            second_chunk = slice(b * BLK + ROW, (b + 1) * BLK)
            state = dot_t(
                kv[b * BLK:(b + 1) * BLK, mine], diagonal(kv[first_chunk, other], kv[second_chunk, other])
            )
            before = total[h]
            within[2 * b, h] = before.astype(BF16)
            middle = before + state[:, :HEAD]
            within[2 * b + 1, h] = middle.astype(BF16)
            total[h] = middle + state[:, HEAD:]
        scores = {}
        for c in range(PER):
            row = b * PER + c
            chunk = slice(row * ROW, (row + 1) * ROW)
            for p in range(HEADS // 2):
                low, high = 2 * p * HEAD, (2 * p + 1) * HEAD
                keys = diagonal(kv[chunk, low:low + HEAD], kv[chunk, high:high + HEAD])
                both = dot_nt(qs[row, :, p * PAIR:(p + 1) * PAIR], keys)
                scores[c, p] = jnp.where(causal, both, 0.0).astype(BF16)
        for c in range(PER):
            row = b * PER + c
            chunk = slice(row * ROW, (row + 1) * ROW)
            for p in range(HEADS // 2):
                low, high = D + 2 * p * HEAD, D + (2 * p + 1) * HEAD
                values = diagonal(kv[chunk, low:low + HEAD], kv[chunk, high:high + HEAD])
                att[row, :, p * PAIR:(p + 1) * PAIR] = dot(scores[c, p], values)

    def within_device(start, stop):
        for b in range(start, stop):
            if b < blocks:
                inputs(b)
            if b > 0:
                local(b - 1)

    cut_one = blocks // 2
    cut_two = blocks - 2
    within_device(0, cut_one)

    def later_copy(t, j):
        return remote(
            quad_send.at[part_rows(j)], quad_recv.at[t - 1, part_rows(j)],
            s2.at[t - 1, j], r2.at[t - 1, j],
            ((quad + t) % quads) * 2 + side, narrow,
        )

    for j in range(PARTS):
        piece = slice(j * PART, (j + 1) * PART)
        for t in range(1, members):
            gather_copy(t, j).wait_recv()
        quad_sum = own_total[place, piece].astype(F32)
        for t in range(1, members):
            quad_sum = quad_sum + quad_parts[t - 1, piece].astype(F32)
        quad_send[piece] = quad_sum.astype(BF16)
        for t in range(1, quads):
            @pl.when(quad + t < quads)
            def _(t=t, j=j):
                later_copy(t, j).start()

    within_device(cut_one, cut_two)
    loads[1].wait()
    mixed[...] = dot(wout[...], wfeat[...]).astype(BF16)

    def assign(b, carry):
        held = [jnp.int32(-1)] * most
        for r in range(rows):
            hit = brick_ref[0, r] == b
            held = [
                jnp.where(hit, jnp.int32(r) if m == 0 else held[m - 1], held[m]) for m in range(most)
            ]
        for m in range(most):
            slots[b * most + m] = held[m]
        return carry

    lax.fori_loop(0, wide_count, assign, 0)

    def spread_copy(t, j):
        other, to_wide, to_narrow = member(t)
        return remote(
            prefix_send.at[other, part_rows(j)], prefix_recv.at[place, part_rows(j)],
            s3.at[t - 1, j], r3.at[t - 1, j], to_wide, to_narrow,
        )

    def spread_arrival(t, j):
        source = (place - t + members) % members
        return remote(
            prefix_send.at[source, part_rows(j)], prefix_recv.at[source, part_rows(j)],
            s3.at[t - 1, j], r3.at[t - 1, j], wide, narrow,
        )

    for j in range(PARTS):
        piece = slice(j * PART, (j + 1) * PART)
        base[piece] = jnp.zeros((PART, HEAD), F32)
        for t in range(1, quads):
            @pl.when(quad - t >= 0)
            def _(t=t, j=j, piece=piece):
                later_copy(t, j).wait_recv()
                base[piece] = base[piece] + quad_recv[t - 1, piece].astype(F32)
        running = base[piece]
        for m in range(members):
            prefix_send[m, piece] = running.astype(BF16)
            if m < members - 1:
                value = own_total[place, piece].astype(F32)
                for t in range(1, members):
                    value = jnp.where(
                        (place - t + members) % members == m,
                        quad_parts[t - 1, piece].astype(F32), value,
                    )
                running = running + value
        for t in range(1, members):
            spread_copy(t, j).start()
        prefix_recv[place, piece] = prefix_send[place, piece]

    within_device(cut_two, blocks + 1)

    for j in range(PARTS):
        for t in range(1, members):
            spread_arrival(t, j).wait_recv()
    for h in range(HEADS):
        total[h] = prefix_recv[h].astype(F32)

    def state_of(row, p):
        return diagonal(*[
            (within[row, 2 * p + i].astype(F32) + total[2 * p + i]).astype(BF16) for i in range(2)
        ])

    def scaled(one):
        square = jnp.mean(one * one, axis=-1, keepdims=True)
        return (one * lax.rsqrt(square + epsilon)).astype(BF16)

    def attend(b):
        for row in range(PER * b, PER * (b + 1)):
            for p in range(HEADS // 2):
                columns = slice(p * PAIR, (p + 1) * PAIR)
                att[row, :, columns] += dot(qs[row, :, columns], state_of(row, p))

    def normalise(b):
        for row in range(PER * b, PER * (b + 1)):
            for h in range(HEADS):
                mine = slice(h * HEAD, (h + 1) * HEAD)
                qs[row, :, mine] = scaled(att[row, :, mine])

    def finish(b):
        span = slice(PER * b, PER * (b + 1))
        normed = qs[span].reshape(BLK, D)
        mine = direct[span].reshape(BLK, PF) + dot(normed, mixed[...])
        feats[span] = mine.astype(BF16).reshape(PER, ROW, PF)

    def project():
        for b in range(blocks + 2):
            if b < blocks:
                attend(b)
            if 0 < b <= blocks:
                normalise(b - 1)
            if b > 1:
                finish(b - 2)

    cell_ids = lax.broadcasted_iota(jnp.int32, (CELLS, ROW), 0)

    def across(r):
        target = wide
        for s in range(bits):
            target = target + (r // 2**s) % 2 * 2**s * (1 - 2 * ((wide // 2**s) % 2))
        return target

    def named_rows(brick):
        marks, chosen = [], []
        for m in range(most):
            named = slots[brick * most + m]
            row = jnp.maximum(named, 0)
            cells = cell_ref[pl.ds(row, 1), :] + jnp.where(named < 0, -CELLS, 0)
            marks.append(jnp.where(cell_ids == cells, 1.0, 0.0).astype(BF16))
            chosen.append(row)
        return jnp.concatenate(marks, axis=1), chosen

    def pool_ready(brick):
        marks, chosen = named_rows(brick)
        return dot(marks, jnp.concatenate([feats[row] for row in chosen], axis=0))

    def pool_afresh(brick):
        marks, chosen = named_rows(brick)
        normed, plain = [], []
        for row in chosen:
            pieces = []
            for p in range(HEADS // 2):
                columns = slice(p * PAIR, (p + 1) * PAIR)
                attended = att[row, :, columns] + dot(qs[row, :, columns], state_of(row, p))
                pieces += [scaled(attended[:, i * HEAD:(i + 1) * HEAD]) for i in range(2)]
            normed.append(jnp.concatenate(pieces, axis=1))
            plain.append(direct[row])
        features = jnp.concatenate(plain, axis=0) + dot(jnp.concatenate(normed, axis=0), mixed[...])
        return dot(marks, features.astype(BF16))

    def piece_copy(label, bit, k):
        span = pl.ds(k * PIECE, PIECE)
        return remote(
            part_send.at[label - 1, span], part_recv.at[label - 1, span],
            sa.at[label - 1, k], ra.at[label - 1, k], across(bit), narrow,
        )

    def send_partner(label, pool):
        part_send[label - 1] = pool.astype(BF16)
        for k in PIECE_ORDER:
            piece_copy(label, 1, k).start()

    def halo_copy(k, dy, dx):
        if dy == 0:
            source = pooled.at[:, pl.ds(BY - EDGE if dx > 0 else 0, EDGE)]
            target = cols_recv.at[0 if dx > 0 else 1]
        else:
            span = pl.ds(BX - HALO if dy > 0 else 0, HALO)
            if dx == 0:
                source = pooled.at[span]
                target = rows_recv.at[0 if dy > 0 else 1]
            else:
                source = pooled.at[span, pl.ds(BY - EDGE if dx > 0 else 0, EDGE)]
                target = corner_recv.at[(0 if dy > 0 else 2) + (0 if dx > 0 else 1)]
        return remote(
            source, target, sh.at[k], rh.at[k],
            (wide + dy + wide_count) % wide_count, (narrow + dx + narrow_count) % narrow_count,
        )

    steps = [(dy, dx) for dy in (-1, 1) for dx in (0, -1, 1)] + [(0, -1), (0, 1)]

    def inside(dy, dx):
        return (
            (wide + dy >= 0) & (wide + dy < wide_count)
            & (narrow + dx >= 0) & (narrow + dx < narrow_count)
        )

    def send_halo(wanted):
        for k, (dy, dx) in enumerate(steps):
            if dy != wanted:
                continue

            @pl.when(inside(dy, dx))
            def _(k=k, dy=dy, dx=dx):
                halo_copy(k, dy, dx).start()

    def pool_own(label):
        own_part[label // 2] = pool_ready(across(label))

    def reduce(label):
        low = label & -label if label else wide_count
        for k in PIECE_ORDER:
            span = slice(k * PIECE, (k + 1) * PIECE)
            summed = own_part[label // 2, span]
            bit = 1
            while bit < low:
                piece_copy(label + bit, bit, k).wait_recv()
                summed = summed + part_recv[label + bit - 1, span].astype(F32)
                bit *= 2
            if label:
                part_send[label - 1, span] = summed.astype(BF16)
                piece_copy(label, low, k).start()
            else:
                lines = slice(k * PIECE // BY, (k + 1) * PIECE // BY)
                done = summed.astype(BF16).reshape(PIECE // BY, BY, PF)
                pooled[lines] = done
                ext[HALO + lines.start:HALO + lines.stop, EDGE:EDGE + BY, :] = done
                if k == 0:
                    send_halo(-1)
                if k == PIECES - 1:
                    send_halo(1)

    top = wide_count - 1
    send_partner(top, pool_afresh(across(top)))
    project()
    send_partner(top - 2, pool_ready(across(top - 2)))
    pool_own(top - 1)
    reduce(top - 1)
    for label in range(top - 4, 0, -2):
        send_partner(label, pool_ready(across(label)))
    for label in range(top - 3, -1, -2):
        pool_own(label)
    for label in range(top - 3, -1, -2):
        reduce(label)
    send_halo(0)

    def take_halo(across_rows):
        for k, (dy, dx) in enumerate(steps):
            if (dy != 0) != across_rows:
                continue

            @pl.when(inside(-dy, -dx))
            def _(k=k, dy=dy, dx=dx):
                halo_copy(k, dy, dx).wait_recv()
                span = slice(HALO, HALO + BX)
                if dy > 0:
                    span = slice(0, HALO)
                elif dy < 0:
                    span = slice(HALO + BX, 2 * HALO + BX)
                if dx == 0:
                    ext[span, EDGE:EDGE + BY, :] = rows_recv[0 if dy > 0 else 1]
                else:
                    columns = slice(0, EDGE) if dx > 0 else slice(EDGE + BY, WIDTH)
                    if dy == 0:
                        ext[span, columns, :] = cols_recv[0 if dx > 0 else 1]
                    else:
                        ext[span, columns, :] = corner_recv[(0 if dy > 0 else 2) + (0 if dx > 0 else 1)]

    def convolve(field, weight, start, height):
        size = height * WIDTH
        result = None
        for dx in range(3):
            shifted = None
            for dy in range(3):
                window = field[start + dy:start + dy + height].reshape(size, PF)
                term = dot(window, weight[dy, dx])
                shifted = term if shifted is None else shifted + term
            if dx != 1:
                shifted = pltpu.roll(shifted, 1 if dx == 0 else size - 1, 0)
            result = shifted if result is None else result + shifted
        return result.reshape(height, WIDTH, PF)

    def first_layer(start, height):
        active = jax.nn.gelu(convolve(ext, first, start, height), approximate=True)
        extent = (height, WIDTH, PF)
        grid_row = lax.broadcasted_iota(jnp.int32, extent, 0) + wide * BX + start - 1
        grid_column = lax.broadcasted_iota(jnp.int32, extent, 1) + narrow * BY - EDGE
        real = (
            (grid_row >= 0) & (grid_row < wide_count * BX)
            & (grid_column >= 0) & (grid_column < narrow_count * BY)
        )
        inner[start:start + height] = jnp.where(real, active, 0.0).astype(BF16)

    def second_layer(start, height):
        out_ref[start:start + height] = convolve(inner, second, start, height)[:, EDGE:EDGE + BY, :]

    loads[3].wait()
    loads[4].wait()
    take_halo(False)
    first_layer(HALO, BX - HALO)
    second_layer(HALO, BX - 2 * HALO)
    take_halo(True)
    first_layer(0, HALO)
    first_layer(BX, HALO)
    second_layer(0, HALO)
    second_layer(BX - HALO, HALO)

    for j in range(PARTS):
        for t in range(1, members):
            gather_copy(t, j).wait_send()
            spread_copy(t, j).wait_send()
        for t in range(1, quads):
            @pl.when(quad + t < quads)
            def _(t=t, j=j):
                later_copy(t, j).wait_send()

    for label in range(1, wide_count):
        for k in range(PIECES):
            piece_copy(label, label & -label, k).wait_send()
    for k, (dy, dx) in enumerate(steps):
        @pl.when(inside(dy, dx))
        def _(k=k, dy=dy, dx=dx):
            halo_copy(k, dy, dx).wait_send()


def per_device(voxels, w_qkv, w_out, w_feature, conv_first, conv_second, row_brick, cell_place):
    token_count = voxels.shape[0]
    rows = token_count // ROW
    wide_count = lax.axis_size("wide")
    narrow_count = lax.axis_size("narrow")
    blocks = token_count // BLK
    quads = wide_count // 2
    members = 2 * narrow_count
    others = max(1, quads - 1)
    most = 2 * (-(-rows // wide_count))
    anywhere = pl.BlockSpec(memory_space=pl.ANY)
    vmem = pl.BlockSpec(memory_space=pltpu.VMEM)
    smem = pl.BlockSpec(memory_space=pltpu.SMEM)
    dma = pltpu.SemaphoreType.DMA
    state = (HEAD, HEAD)
    grid = (CELLS, PF)
    scratch = [
        pltpu.VMEM(voxels.shape, BF16),
        pltpu.VMEM(w_qkv.shape, BF16),
        pltpu.VMEM(w_out.shape, BF16),
        pltpu.VMEM(w_feature.shape, BF16),
        pltpu.VMEM(conv_first.shape, BF16),
        pltpu.VMEM(conv_second.shape, BF16),
        pltpu.VMEM((token_count, 2 * D), BF16),
        pltpu.VMEM((rows, ROW, D), BF16),
        pltpu.VMEM((rows, ROW, D), F32),
        pltpu.VMEM((rows, ROW, PF), F32),
        pltpu.VMEM((D, PF), BF16),
        pltpu.VMEM((rows, HEADS) + state, BF16),
        pltpu.VMEM((HEADS,) + state, F32),
        pltpu.VMEM((rows, ROW, PF), BF16),
        pltpu.SMEM((wide_count * most,), jnp.int32),
        pltpu.VMEM((MIDDLE, D), F32),
        pltpu.VMEM((MIDDLE, MIDDLE), F32),
        pltpu.VMEM((D, D), BF16),
        pltpu.VMEM(state, F32),
        pltpu.VMEM((members,) + state, BF16),
        pltpu.VMEM((members,) + state, BF16),
        pltpu.VMEM(state, BF16),
        pltpu.VMEM((others,) + state, BF16),
        pltpu.VMEM((members,) + state, BF16),
        pltpu.VMEM((members,) + state, BF16),
        pltpu.VMEM((wide_count - 1,) + grid, BF16),
        pltpu.VMEM((wide_count - 1,) + grid, BF16),
        pltpu.VMEM((quads,) + grid, F32),
        pltpu.VMEM((BX, BY, PF), BF16),
        pltpu.VMEM((BX + 2 * HALO, WIDTH, PF), BF16),
        pltpu.VMEM((2, HALO, BY, PF), BF16),
        pltpu.VMEM((2, BX, EDGE, PF), BF16),
        pltpu.VMEM((4, HALO, EDGE, PF), BF16),
        pltpu.VMEM((BX + 2, WIDTH, PF), BF16),
        dma((blocks,)),
        dma((6,)),
        dma((members - 1, PARTS)), dma((members - 1, PARTS)),
        dma((others, PARTS)), dma((others, PARTS)),
        dma((members - 1, PARTS)), dma((members - 1, PARTS)),
        dma((wide_count - 1, PIECES)), dma((wide_count - 1, PIECES)),
        dma((8,)), dma((8,)),
    ]
    return pl.pallas_call(
        functools.partial(kernel, wide_count, narrow_count, token_count, most),
        out_shape=jax.ShapeDtypeStruct((BX, BY, PF), F32),
        in_specs=[anywhere] * 6 + [smem, vmem],
        out_specs=vmem,
        scratch_shapes=scratch,
        compiler_params=pltpu.CompilerParams(
            collective_id=0, has_side_effects=True, vmem_limit_bytes=56 * 1024 * 1024
        ),
        name="scene_flow",
    )(
        voxels, w_qkv, w_out, w_feature, conv_first, conv_second,
        row_brick.reshape(1, rows), cell_place.reshape(rows, ROW),
    )


def solution(mesh):
    placed = (
        P(("group", "wide", "narrow"), None),
        P(),
        P(),
        P(),
        P(),
        P(),
        P(("group", "wide", "narrow"), None),
        P(("group", "wide", "narrow")),
    )
    return jax.shard_map(
        per_device,
        mesh=mesh,
        in_specs=placed,
        out_specs=P(("group", "wide"), "narrow", None),
        check_vma=False,
    )
```

```python
import functools
import math

import jax
import jax.numpy as jnp
from jax import lax
from jax.experimental import pallas as pl
from jax.experimental.pallas import tpu as pltpu
from jax.sharding import PartitionSpec as P

D = 512
HEADS = 4
HEAD = 128
PF = 256
ROW = 128
BLK = 256
PER = BLK // ROW
BX = 8
BY = 32
CELLS = BX * BY
PAIR = 2 * HEAD
EDGE = 8
MIDDLE = D // 2
WIDTH = BY + 2 * EDGE
HALO = 2
PIECES = 4
PIECE = CELLS // PIECES
PIECE_ORDER = (0, 3, 1, 2)
PARTS = 2
PART = HEAD // PARTS

epsilon = 1e-06
MESH = pl.DeviceIdType.MESH
F32 = jnp.float32
BF16 = jnp.bfloat16


def dot(a, b):
    return jnp.dot(a, b, preferred_element_type=F32)


def dot_t(a, b):
    return lax.dot_general(a, b, (((0,), (0,)), ((), ())), preferred_element_type=F32)


def dot_nt(a, b):
    return lax.dot_general(a, b, (((1,), (1,)), ((), ())), preferred_element_type=F32)


def diagonal(upper, lower):
    blank_right = jnp.zeros((upper.shape[0], lower.shape[1]), upper.dtype)
    blank_left = jnp.zeros((lower.shape[0], upper.shape[1]), lower.dtype)
    return jnp.concatenate(
        [
            jnp.concatenate([upper, blank_right], axis=1),
            jnp.concatenate([blank_left, lower], axis=1),
        ],
        axis=0,
    )


def kernel(
    wide_count, narrow_count, token_count, most,
    vox_hbm, wqkv_hbm, wout_hbm, wfeat_hbm, first_hbm, second_hbm, brick_ref, cell_ref,
    out_ref,
    vox, wqkv, wout, wfeat, first, second,
    kv, qs, att, direct, mixed, within, total, feats, slots, gram_upper, gram_lower, seen, base,
    own_total, quad_parts, quad_send, quad_recv, prefix_send, prefix_recv,
    part_send, part_recv, own_part,
    pooled, ext, rows_recv, cols_recv, corner_recv, inner,
    vox_sem, load_sem,
    s1, r1, s2, r2, s3, r3, sa, ra, sh, rh,
):
    blocks = token_count // BLK
    rows = token_count // ROW
    quads = wide_count // 2
    bits = wide_count.bit_length() - 1
    wide = lax.axis_index("wide")
    narrow = lax.axis_index("narrow")
    side = wide % 2
    quad = wide // 2
    members = 2 * narrow_count
    place = side * narrow_count + narrow

    def load_vox(b):
        span = pl.ds(pl.multiple_of(b * BLK, BLK), BLK)
        return pltpu.make_async_copy(vox_hbm.at[span], vox.at[span], vox_sem.at[b])

    def load(source, target, k):
        return pltpu.make_async_copy(source, target, load_sem.at[k])

    loads = [
        load(wqkv_hbm.at[:, pl.ds(D, 2 * D)], wqkv.at[:, pl.ds(D, 2 * D)], 0),
        load(wout_hbm, wout, 1),
        load(wfeat_hbm, wfeat, 2),
        load(first_hbm, first, 3),
        load(second_hbm, second, 4),
        load(wqkv_hbm.at[:, pl.ds(0, D)], wqkv.at[:, pl.ds(0, D)], 5),
    ]
    for b in range(blocks):
        load_vox(b).start()
    for k in (0, 5, 2, 1, 3, 4):
        loads[k].start()

    barrier = pltpu.get_barrier_semaphore()
    beside = (wide + wide_count + 2 * side - 1) % wide_count
    partners = [
        (quad * 2 + (place + t) % members // narrow_count, (place + t) % narrow_count)
        for t in range(1, members)
    ]
    partners += [((quad + t) % quads * 2 + side, narrow) for t in range(1, quads)]
    partners += [(beside, n) for n in range(narrow_count)]
    for to_wide, to_narrow in partners:
        pl.semaphore_signal(
            barrier, inc=1, device_id={"wide": to_wide, "narrow": to_narrow}, device_id_type=MESH
        )

    def remote(source, target, send_sem, recv_sem, to_wide, to_narrow):
        return pltpu.make_async_remote_copy(
            src_ref=source, dst_ref=target, send_sem=send_sem, recv_sem=recv_sem,
            device_id={"wide": to_wide, "narrow": to_narrow}, device_id_type=MESH,
        )

    causal = lax.broadcasted_iota(jnp.int32, (ROW, PAIR), 0) >= (
        lax.broadcasted_iota(jnp.int32, (ROW, PAIR), 1) % ROW
    )
    total[...] = jnp.zeros_like(total)
    ext[...] = jnp.zeros_like(ext)

    def gram(start, stop):
        span = slice(start, stop)
        upper = dot_t(vox[span, :MIDDLE], vox[span, :])
        lower = dot_t(vox[span, MIDDLE:], vox[span, MIDDLE:])
        return upper, lower

    half = token_count // 2
    for b in range(blocks // 2):
        load_vox(b).wait()
    gram_upper[...], gram_lower[...] = gram(0, half)
    for b in range(blocks // 2, blocks):
        load_vox(b).wait()
    upper, lower = gram(half, token_count)
    upper = (gram_upper[...] + upper).astype(BF16)
    lower = (gram_lower[...] + lower).astype(BF16)
    loads[0].wait()
    seen[:MIDDLE] = dot(upper, wqkv[:, 2 * D:]).astype(BF16)
    seen[MIDDLE:] = (
        dot_t(upper[:, MIDDLE:], wqkv[:MIDDLE, 2 * D:]) + dot(lower, wqkv[MIDDLE:, 2 * D:])
    ).astype(BF16)
    for p in range(HEADS // 2):
        columns = slice(p * PAIR, (p + 1) * PAIR)
        state = dot_t(wqkv[:, D + p * PAIR:D + (p + 1) * PAIR], seen[:, columns])
        for i in range(2):
            corner = slice(i * HEAD, (i + 1) * HEAD)
            own_total[2 * p + i] = state[corner, corner].astype(BF16)
    pl.semaphore_wait(barrier, len(partners))

    def part_rows(j):
        return pl.ds(j * PART, PART)

    def member(t):
        other = (place + t) % members
        return other, quad * 2 + other // narrow_count, other % narrow_count

    def gather_copy(t, j):
        other, to_wide, to_narrow = member(t)
        return remote(
            own_total.at[other, part_rows(j)], quad_parts.at[t - 1, part_rows(j)],
            s1.at[t - 1, j], r1.at[t - 1, j], to_wide, to_narrow,
        )

    for j in range(PARTS):
        for t in range(1, members):
            gather_copy(t, j).start()

    def inputs(b):
        span = slice(b * BLK, (b + 1) * BLK)
        if b == 0:
            loads[5].wait()
            loads[2].wait()
        kv[span, :] = dot(vox[span, :], wqkv[:, D:]).astype(BF16)
        query = dot(vox[span, :], wqkv[:, :D]).astype(BF16)
        qs[PER * b:PER * (b + 1)] = query.reshape(PER, ROW, D)
        direct[PER * b:PER * (b + 1)] = dot(vox[span, :], wfeat[...]).reshape(PER, ROW, PF)

    def local(b):
        for h in range(HEADS):
            mine = slice(h * HEAD, (h + 1) * HEAD)
            other = slice(D + h * HEAD, D + (h + 1) * HEAD)
            first_chunk = slice(b * BLK, b * BLK + ROW)
            second_chunk = slice(b * BLK + ROW, (b + 1) * BLK)
            state = dot_t(
                kv[b * BLK:(b + 1) * BLK, mine], diagonal(kv[first_chunk, other], kv[second_chunk, other])
            )
            before = total[h]
            within[2 * b, h] = before.astype(BF16)
            middle = before + state[:, :HEAD]
            within[2 * b + 1, h] = middle.astype(BF16)
            total[h] = middle + state[:, HEAD:]
        scores = {}
        for c in range(PER):
            row = b * PER + c
            chunk = slice(row * ROW, (row + 1) * ROW)
            for p in range(HEADS // 2):
                low, high = 2 * p * HEAD, (2 * p + 1) * HEAD
                keys = diagonal(kv[chunk, low:low + HEAD], kv[chunk, high:high + HEAD])
                both = dot_nt(qs[row, :, p * PAIR:(p + 1) * PAIR], keys)
                scores[c, p] = jnp.where(causal, both, 0.0).astype(BF16)
        for c in range(PER):
            row = b * PER + c
            chunk = slice(row * ROW, (row + 1) * ROW)
            for p in range(HEADS // 2):
                low, high = D + 2 * p * HEAD, D + (2 * p + 1) * HEAD
                values = diagonal(kv[chunk, low:low + HEAD], kv[chunk, high:high + HEAD])
                att[row, :, p * PAIR:(p + 1) * PAIR] = dot(scores[c, p], values)

    def within_device(start, stop):
        for b in range(start, stop):
            if b < blocks:
                inputs(b)
            if b > 0:
                local(b - 1)

    cut_one = blocks // 2
    cut_two = blocks - 2
    within_device(0, cut_one)

    def later_copy(t, j):
        return remote(
            quad_send.at[part_rows(j)], quad_recv.at[t - 1, part_rows(j)],
            s2.at[t - 1, j], r2.at[t - 1, j],
            ((quad + t) % quads) * 2 + side, narrow,
        )

    for j in range(PARTS):
        piece = slice(j * PART, (j + 1) * PART)
        for t in range(1, members):
            gather_copy(t, j).wait_recv()
        quad_sum = own_total[place, piece].astype(F32)
        for t in range(1, members):
            quad_sum = quad_sum + quad_parts[t - 1, piece].astype(F32)
        quad_send[piece] = quad_sum.astype(BF16)
        for t in range(1, quads):
            @pl.when(quad + t < quads)
            def _(t=t, j=j):
                later_copy(t, j).start()

    within_device(cut_one, cut_two)
    loads[1].wait()
    mixed[...] = dot(wout[...], wfeat[...]).astype(BF16)

    def assign(b, carry):
        held = [jnp.int32(-1)] * most
        for r in range(rows):
            hit = brick_ref[0, r] == b
            held = [
                jnp.where(hit, jnp.int32(r) if m == 0 else held[m - 1], held[m]) for m in range(most)
            ]
        for m in range(most):
            slots[b * most + m] = held[m]
        return carry

    lax.fori_loop(0, wide_count, assign, 0)

    def spread_copy(t, j):
        other, to_wide, to_narrow = member(t)
        return remote(
            prefix_send.at[other, part_rows(j)], prefix_recv.at[place, part_rows(j)],
            s3.at[t - 1, j], r3.at[t - 1, j], to_wide, to_narrow,
        )

    def spread_arrival(t, j):
        source = (place - t + members) % members
        return remote(
            prefix_send.at[source, part_rows(j)], prefix_recv.at[source, part_rows(j)],
            s3.at[t - 1, j], r3.at[t - 1, j], wide, narrow,
        )

    for j in range(PARTS):
        piece = slice(j * PART, (j + 1) * PART)
        base[piece] = jnp.zeros((PART, HEAD), F32)
        for t in range(1, quads):
            @pl.when(quad - t >= 0)
            def _(t=t, j=j, piece=piece):
                later_copy(t, j).wait_recv()
                base[piece] = base[piece] + quad_recv[t - 1, piece].astype(F32)
        running = base[piece]
        for m in range(members):
            prefix_send[m, piece] = running.astype(BF16)
            if m < members - 1:
                value = own_total[place, piece].astype(F32)
                for t in range(1, members):
                    value = jnp.where(
                        (place - t + members) % members == m,
                        quad_parts[t - 1, piece].astype(F32), value,
                    )
                running = running + value
        for t in range(1, members):
            spread_copy(t, j).start()
        prefix_recv[place, piece] = prefix_send[place, piece]

    within_device(cut_two, blocks + 1)

    for j in range(PARTS):
        for t in range(1, members):
            spread_arrival(t, j).wait_recv()
    for h in range(HEADS):
        total[h] = prefix_recv[h].astype(F32)

    def state_of(row, p):
        return diagonal(*[
            (within[row, 2 * p + i].astype(F32) + total[2 * p + i]).astype(BF16) for i in range(2)
        ])

    def scaled(one):
        square = jnp.mean(one * one, axis=-1, keepdims=True)
        return (one * lax.rsqrt(square + epsilon)).astype(BF16)

    def attend(b):
        for row in range(PER * b, PER * (b + 1)):
            for p in range(HEADS // 2):
                columns = slice(p * PAIR, (p + 1) * PAIR)
                att[row, :, columns] += dot(qs[row, :, columns], state_of(row, p))

    def normalise(b):
        for row in range(PER * b, PER * (b + 1)):
            for h in range(HEADS):
                mine = slice(h * HEAD, (h + 1) * HEAD)
                qs[row, :, mine] = scaled(att[row, :, mine])

    def finish(b):
        span = slice(PER * b, PER * (b + 1))
        normed = qs[span].reshape(BLK, D)
        mine = direct[span].reshape(BLK, PF) + dot(normed, mixed[...])
        feats[span] = mine.astype(BF16).reshape(PER, ROW, PF)

    def project():
        for b in range(blocks + 2):
            if b < blocks:
                attend(b)
            if 0 < b <= blocks:
                normalise(b - 1)
            if b > 1:
                finish(b - 2)

    cell_ids = lax.broadcasted_iota(jnp.int32, (CELLS, ROW), 0)

    def across(r):
        target = wide
        for s in range(bits):
            target = target + (r // 2**s) % 2 * 2**s * (1 - 2 * ((wide // 2**s) % 2))
        return target

    def named_rows(brick):
        marks, chosen = [], []
        for m in range(most):
            named = slots[brick * most + m]
            row = jnp.maximum(named, 0)
            cells = cell_ref[pl.ds(row, 1), :] + jnp.where(named < 0, -CELLS, 0)
            marks.append(jnp.where(cell_ids == cells, 1.0, 0.0).astype(BF16))
            chosen.append(row)
        return jnp.concatenate(marks, axis=1), chosen

    def pool_ready(brick):
        marks, chosen = named_rows(brick)
        return dot(marks, jnp.concatenate([feats[row] for row in chosen], axis=0))

    def pool_afresh(brick):
        marks, chosen = named_rows(brick)
        normed, plain = [], []
        for row in chosen:
            pieces = []
            for p in range(HEADS // 2):
                columns = slice(p * PAIR, (p + 1) * PAIR)
                attended = att[row, :, columns] + dot(qs[row, :, columns], state_of(row, p))
                pieces += [scaled(attended[:, i * HEAD:(i + 1) * HEAD]) for i in range(2)]
            normed.append(jnp.concatenate(pieces, axis=1))
            plain.append(direct[row])
        features = jnp.concatenate(plain, axis=0) + dot(jnp.concatenate(normed, axis=0), mixed[...])
        return dot(marks, features.astype(BF16))

    def piece_copy(label, bit, k):
        span = pl.ds(k * PIECE, PIECE)
        return remote(
            part_send.at[label - 1, span], part_recv.at[label - 1, span],
            sa.at[label - 1, k], ra.at[label - 1, k], across(bit), narrow,
        )

    def send_partner(label, pool):
        part_send[label - 1] = pool.astype(BF16)
        for k in PIECE_ORDER:
            piece_copy(label, 1, k).start()

    def halo_copy(k, dy, dx):
        if dy == 0:
            source = pooled.at[:, pl.ds(BY - EDGE if dx > 0 else 0, EDGE)]
            target = cols_recv.at[0 if dx > 0 else 1]
        else:
            span = pl.ds(BX - HALO if dy > 0 else 0, HALO)
            if dx == 0:
                source = pooled.at[span]
                target = rows_recv.at[0 if dy > 0 else 1]
            else:
                source = pooled.at[span, pl.ds(BY - EDGE if dx > 0 else 0, EDGE)]
                target = corner_recv.at[(0 if dy > 0 else 2) + (0 if dx > 0 else 1)]
        return remote(
            source, target, sh.at[k], rh.at[k],
            (wide + dy + wide_count) % wide_count, (narrow + dx + narrow_count) % narrow_count,
        )

    steps = [(dy, dx) for dy in (-1, 1) for dx in (0, -1, 1)] + [(0, -1), (0, 1)]

    def inside(dy, dx):
        return (
            (wide + dy >= 0) & (wide + dy < wide_count)
            & (narrow + dx >= 0) & (narrow + dx < narrow_count)
        )

    def send_halo(wanted):
        for k, (dy, dx) in enumerate(steps):
            if dy != wanted:
                continue

            @pl.when(inside(dy, dx))
            def _(k=k, dy=dy, dx=dx):
                halo_copy(k, dy, dx).start()

    def pool_own(label):
        own_part[label // 2] = pool_ready(across(label))

    def reduce(label):
        low = label & -label if label else wide_count
        for k in PIECE_ORDER:
            span = slice(k * PIECE, (k + 1) * PIECE)
            summed = own_part[label // 2, span]
            bit = 1
            while bit < low:
                piece_copy(label + bit, bit, k).wait_recv()
                summed = summed + part_recv[label + bit - 1, span].astype(F32)
                bit *= 2
            if label:
                part_send[label - 1, span] = summed.astype(BF16)
                piece_copy(label, low, k).start()
            else:
                lines = slice(k * PIECE // BY, (k + 1) * PIECE // BY)
                done = summed.astype(BF16).reshape(PIECE // BY, BY, PF)
                pooled[lines] = done
                ext[HALO + lines.start:HALO + lines.stop, EDGE:EDGE + BY, :] = done
                if k == 0:
                    send_halo(-1)
                if k == PIECES - 1:
                    send_halo(1)

    top = wide_count - 1
    send_partner(top, pool_afresh(across(top)))
    project()
    send_partner(top - 2, pool_ready(across(top - 2)))
    pool_own(top - 1)
    reduce(top - 1)
    for label in range(top - 4, 0, -2):
        send_partner(label, pool_ready(across(label)))
    for label in range(top - 3, -1, -2):
        pool_own(label)
    for label in range(top - 3, -1, -2):
        reduce(label)
    send_halo(0)

    def take_halo(across_rows):
        for k, (dy, dx) in enumerate(steps):
            if (dy != 0) != across_rows:
                continue

            @pl.when(inside(-dy, -dx))
            def _(k=k, dy=dy, dx=dx):
                halo_copy(k, dy, dx).wait_recv()
                span = slice(HALO, HALO + BX)
                if dy > 0:
                    span = slice(0, HALO)
                elif dy < 0:
                    span = slice(HALO + BX, 2 * HALO + BX)
                if dx == 0:
                    ext[span, EDGE:EDGE + BY, :] = rows_recv[0 if dy > 0 else 1]
                else:
                    columns = slice(0, EDGE) if dx > 0 else slice(EDGE + BY, WIDTH)
                    if dy == 0:
                        ext[span, columns, :] = cols_recv[0 if dx > 0 else 1]
                    else:
                        ext[span, columns, :] = corner_recv[(0 if dy > 0 else 2) + (0 if dx > 0 else 1)]

    def convolve(field, weight, start, height):
        size = height * WIDTH
        result = None
        for dx in range(3):
            shifted = None
            for dy in range(3):
                window = field[start + dy:start + dy + height].reshape(size, PF)
                term = dot(window, weight[dy, dx])
                shifted = term if shifted is None else shifted + term
            if dx != 1:
                shifted = pltpu.roll(shifted, 1 if dx == 0 else size - 1, 0)
            result = shifted if result is None else result + shifted
        return result.reshape(height, WIDTH, PF)

    def first_layer(start, height):
        active = jax.nn.gelu(convolve(ext, first, start, height), approximate=True)
        extent = (height, WIDTH, PF)
        grid_row = lax.broadcasted_iota(jnp.int32, extent, 0) + wide * BX + start - 1
        grid_column = lax.broadcasted_iota(jnp.int32, extent, 1) + narrow * BY - EDGE
        real = (
            (grid_row >= 0) & (grid_row < wide_count * BX)
            & (grid_column >= 0) & (grid_column < narrow_count * BY)
        )
        inner[start:start + height] = jnp.where(real, active, 0.0).astype(BF16)

    def second_layer(start, height):
        out_ref[start:start + height] = convolve(inner, second, start, height)[:, EDGE:EDGE + BY, :]

    loads[3].wait()
    loads[4].wait()
    take_halo(False)
    first_layer(HALO, BX - HALO)
    second_layer(HALO, BX - 2 * HALO)
    take_halo(True)
    first_layer(0, HALO)
    first_layer(BX, HALO)
    second_layer(0, HALO)
    second_layer(BX - HALO, HALO)

    for j in range(PARTS):
        for t in range(1, members):
            gather_copy(t, j).wait_send()
            spread_copy(t, j).wait_send()
        for t in range(1, quads):
            @pl.when(quad + t < quads)
            def _(t=t, j=j):
                later_copy(t, j).wait_send()

    for label in range(1, wide_count):
        for k in range(PIECES):
            piece_copy(label, label & -label, k).wait_send()
    for k, (dy, dx) in enumerate(steps):
        @pl.when(inside(dy, dx))
        def _(k=k, dy=dy, dx=dx):
            halo_copy(k, dy, dx).wait_send()


def per_device(voxels, w_qkv, w_out, w_feature, conv_first, conv_second, row_brick, cell_place):
    token_count = voxels.shape[0]
    rows = token_count // ROW
    wide_count = lax.axis_size("wide")
    narrow_count = lax.axis_size("narrow")
    blocks = token_count // BLK
    quads = wide_count // 2
    members = 2 * narrow_count
    others = max(1, quads - 1)
    most = 2 * (-(-rows // wide_count))
    anywhere = pl.BlockSpec(memory_space=pl.ANY)
    vmem = pl.BlockSpec(memory_space=pltpu.VMEM)
    smem = pl.BlockSpec(memory_space=pltpu.SMEM)
    dma = pltpu.SemaphoreType.DMA
    state = (HEAD, HEAD)
    grid = (CELLS, PF)
    scratch = [
        pltpu.VMEM(voxels.shape, BF16),
        pltpu.VMEM(w_qkv.shape, BF16),
        pltpu.VMEM(w_out.shape, BF16),
        pltpu.VMEM(w_feature.shape, BF16),
        pltpu.VMEM(conv_first.shape, BF16),
        pltpu.VMEM(conv_second.shape, BF16),
        pltpu.VMEM((token_count, 2 * D), BF16),
        pltpu.VMEM((rows, ROW, D), BF16),
        pltpu.VMEM((rows, ROW, D), F32),
        pltpu.VMEM((rows, ROW, PF), F32),
        pltpu.VMEM((D, PF), BF16),
        pltpu.VMEM((rows, HEADS) + state, BF16),
        pltpu.VMEM((HEADS,) + state, F32),
        pltpu.VMEM((rows, ROW, PF), BF16),
        pltpu.SMEM((wide_count * most,), jnp.int32),
        pltpu.VMEM((MIDDLE, D), F32),
        pltpu.VMEM((MIDDLE, MIDDLE), F32),
        pltpu.VMEM((D, D), BF16),
        pltpu.VMEM(state, F32),
        pltpu.VMEM((members,) + state, BF16),
        pltpu.VMEM((members,) + state, BF16),
        pltpu.VMEM(state, BF16),
        pltpu.VMEM((others,) + state, BF16),
        pltpu.VMEM((members,) + state, BF16),
        pltpu.VMEM((members,) + state, BF16),
        pltpu.VMEM((wide_count - 1,) + grid, BF16),
        pltpu.VMEM((wide_count - 1,) + grid, BF16),
        pltpu.VMEM((quads,) + grid, F32),
        pltpu.VMEM((BX, BY, PF), BF16),
        pltpu.VMEM((BX + 2 * HALO, WIDTH, PF), BF16),
        pltpu.VMEM((2, HALO, BY, PF), BF16),
        pltpu.VMEM((2, BX, EDGE, PF), BF16),
        pltpu.VMEM((4, HALO, EDGE, PF), BF16),
        pltpu.VMEM((BX + 2, WIDTH, PF), BF16),
        dma((blocks,)),
        dma((6,)),
        dma((members - 1, PARTS)), dma((members - 1, PARTS)),
        dma((others, PARTS)), dma((others, PARTS)),
        dma((members - 1, PARTS)), dma((members - 1, PARTS)),
        dma((wide_count - 1, PIECES)), dma((wide_count - 1, PIECES)),
        dma((8,)), dma((8,)),
    ]
    return pl.pallas_call(
        functools.partial(kernel, wide_count, narrow_count, token_count, most),
        out_shape=jax.ShapeDtypeStruct((BX, BY, PF), F32),
        in_specs=[anywhere] * 6 + [smem, vmem],
        out_specs=vmem,
        scratch_shapes=scratch,
        compiler_params=pltpu.CompilerParams(
            collective_id=0, has_side_effects=True, vmem_limit_bytes=56 * 1024 * 1024
        ),
        name="scene_flow",
    )(
        voxels, w_qkv, w_out, w_feature, conv_first, conv_second,
        row_brick.reshape(1, rows), cell_place.reshape(rows, ROW),
    )


def solution(mesh):
    placed = (
        P(("group", "wide", "narrow"), None),
        P(),
        P(),
        P(),
        P(),
        P(),
        P(("group", "wide", "narrow"), None),
        P(("group", "wide", "narrow")),
    )
    return jax.shard_map(
        per_device,
        mesh=mesh,
        in_specs=placed,
        out_specs=P(("group", "wide"), "narrow", None),
        check_vma=False,
    )
```

```python
import functools
import math

import jax
import jax.numpy as jnp
from jax import lax
from jax.experimental import pallas as pl
from jax.experimental.pallas import tpu as pltpu
from jax.sharding import PartitionSpec as P

D = 512
HEADS = 4
HEAD = 128
PF = 256
ROW = 128
BLK = 256
PER = BLK // ROW
BX = 8
BY = 32
CELLS = BX * BY
PAIR = 2 * HEAD
EDGE = 8
MIDDLE = D // 2
WIDTH = BY + 2 * EDGE
HALO = 2
PIECES = 4
PIECE = CELLS // PIECES
PIECE_ORDER = (0, 3, 1, 2)
PARTS = 2
PART = HEAD // PARTS

epsilon = 1e-06
MESH = pl.DeviceIdType.MESH
F32 = jnp.float32
BF16 = jnp.bfloat16


def dot(a, b):
    return jnp.dot(a, b, preferred_element_type=F32)


def dot_t(a, b):
    return lax.dot_general(a, b, (((0,), (0,)), ((), ())), preferred_element_type=F32)


def dot_nt(a, b):
    return lax.dot_general(a, b, (((1,), (1,)), ((), ())), preferred_element_type=F32)


def diagonal(upper, lower):
    blank_right = jnp.zeros((upper.shape[0], lower.shape[1]), upper.dtype)
    blank_left = jnp.zeros((lower.shape[0], upper.shape[1]), lower.dtype)
    return jnp.concatenate(
        [
            jnp.concatenate([upper, blank_right], axis=1),
            jnp.concatenate([blank_left, lower], axis=1),
        ],
        axis=0,
    )


def kernel(
    wide_count, narrow_count, token_count, most,
    vox_hbm, wqkv_hbm, wout_hbm, wfeat_hbm, first_hbm, second_hbm, brick_ref, cell_ref,
    out_ref,
    vox, wqkv, wout, wfeat, first, second,
    kv, qs, att, direct, mixed, within, total, feats, slots, gram_upper, gram_lower, seen, base, early,
    own_total, quad_parts, quad_send, quad_recv, prefix_send, prefix_recv,
    part_send, part_recv, own_part,
    pooled, ext, rows_recv, cols_recv, corner_recv, inner,
    vox_sem, load_sem,
    s1, r1, s2, r2, s3, r3, sa, ra, sh, rh,
):
    blocks = token_count // BLK
    rows = token_count // ROW
    quads = wide_count // 2
    bits = wide_count.bit_length() - 1
    wide = lax.axis_index("wide")
    narrow = lax.axis_index("narrow")
    side = wide % 2
    quad = wide // 2
    members = 2 * narrow_count
    place = side * narrow_count + narrow

    def load_vox(b):
        span = pl.ds(pl.multiple_of(b * BLK, BLK), BLK)
        return pltpu.make_async_copy(vox_hbm.at[span], vox.at[span], vox_sem.at[b])

    def load(source, target, k):
        return pltpu.make_async_copy(source, target, load_sem.at[k])

    loads = [
        load(wqkv_hbm.at[:, pl.ds(D, 2 * D)], wqkv.at[:, pl.ds(D, 2 * D)], 0),
        load(wout_hbm, wout, 1),
        load(wfeat_hbm, wfeat, 2),
        load(first_hbm, first, 3),
        load(second_hbm, second, 4),
        load(wqkv_hbm.at[:, pl.ds(0, D)], wqkv.at[:, pl.ds(0, D)], 5),
    ]
    for b in range(blocks):
        load_vox(b).start()
    for k in (0, 5, 2, 1, 3, 4):
        loads[k].start()

    barrier = pltpu.get_barrier_semaphore()
    beside = (wide + wide_count + 2 * side - 1) % wide_count
    partners = [
        (quad * 2 + (place + t) % members // narrow_count, (place + t) % narrow_count)
        for t in range(1, members)
    ]
    partners += [((quad + t) % quads * 2 + side, narrow) for t in range(1, quads)]
    partners += [(beside, n) for n in range(narrow_count)]
    for to_wide, to_narrow in partners:
        pl.semaphore_signal(
            barrier, inc=1, device_id={"wide": to_wide, "narrow": to_narrow}, device_id_type=MESH
        )

    def remote(source, target, send_sem, recv_sem, to_wide, to_narrow):
        return pltpu.make_async_remote_copy(
            src_ref=source, dst_ref=target, send_sem=send_sem, recv_sem=recv_sem,
            device_id={"wide": to_wide, "narrow": to_narrow}, device_id_type=MESH,
        )

    causal = lax.broadcasted_iota(jnp.int32, (ROW, PAIR), 0) >= (
        lax.broadcasted_iota(jnp.int32, (ROW, PAIR), 1) % ROW
    )
    total[...] = jnp.zeros_like(total)
    ext[...] = jnp.zeros_like(ext)

    def gram(start, stop):
        span = slice(start, stop)
        upper = dot_t(vox[span, :MIDDLE], vox[span, :])
        lower = dot_t(vox[span, MIDDLE:], vox[span, MIDDLE:])
        return upper, lower

    half = token_count // 2
    for b in range(blocks // 2):
        load_vox(b).wait()
    gram_upper[...], gram_lower[...] = gram(0, half)
    for b in range(blocks // 2, blocks):
        load_vox(b).wait()
    upper, lower = gram(half, token_count)
    upper = (gram_upper[...] + upper).astype(BF16)
    lower = (gram_lower[...] + lower).astype(BF16)
    loads[0].wait()
    seen[:MIDDLE] = dot(upper, wqkv[:, 2 * D:]).astype(BF16)
    seen[MIDDLE:] = (
        dot_t(upper[:, MIDDLE:], wqkv[:MIDDLE, 2 * D:]) + dot(lower, wqkv[MIDDLE:, 2 * D:])
    ).astype(BF16)
    for p in range(HEADS // 2):
        columns = slice(p * PAIR, (p + 1) * PAIR)
        state = dot_t(wqkv[:, D + p * PAIR:D + (p + 1) * PAIR], seen[:, columns])
        for i in range(2):
            corner = slice(i * HEAD, (i + 1) * HEAD)
            own_total[2 * p + i] = state[corner, corner].astype(BF16)
    pl.semaphore_wait(barrier, len(partners))

    def part_rows(j):
        return pl.ds(j * PART, PART)

    def member(t):
        other = (place + t) % members
        return other, quad * 2 + other // narrow_count, other % narrow_count

    def gather_copy(t, j):
        other, to_wide, to_narrow = member(t)
        return remote(
            own_total.at[other, part_rows(j)], quad_parts.at[t - 1, part_rows(j)],
            s1.at[t - 1, j], r1.at[t - 1, j], to_wide, to_narrow,
        )

    for j in range(PARTS):
        for t in range(1, members):
            gather_copy(t, j).start()

    def inputs(b):
        span = slice(b * BLK, (b + 1) * BLK)
        if b == 0:
            loads[5].wait()
            loads[2].wait()
        kv[span, :] = dot(vox[span, :], wqkv[:, D:]).astype(BF16)
        query = dot(vox[span, :], wqkv[:, :D]).astype(BF16)
        qs[PER * b:PER * (b + 1)] = query.reshape(PER, ROW, D)
        direct[PER * b:PER * (b + 1)] = dot(vox[span, :], wfeat[...]).reshape(PER, ROW, PF)

    def local(b):
        for h in range(HEADS):
            mine = slice(h * HEAD, (h + 1) * HEAD)
            other = slice(D + h * HEAD, D + (h + 1) * HEAD)
            first_chunk = slice(b * BLK, b * BLK + ROW)
            second_chunk = slice(b * BLK + ROW, (b + 1) * BLK)
            state = dot_t(
                kv[b * BLK:(b + 1) * BLK, mine], diagonal(kv[first_chunk, other], kv[second_chunk, other])
            )
            before = total[h]
            within[2 * b, h] = before.astype(BF16)
            middle = before + state[:, :HEAD]
            within[2 * b + 1, h] = middle.astype(BF16)
            total[h] = middle + state[:, HEAD:]
        scores = {}
        for c in range(PER):
            row = b * PER + c
            chunk = slice(row * ROW, (row + 1) * ROW)
            for p in range(HEADS // 2):
                low, high = 2 * p * HEAD, (2 * p + 1) * HEAD
                keys = diagonal(kv[chunk, low:low + HEAD], kv[chunk, high:high + HEAD])
                both = dot_nt(qs[row, :, p * PAIR:(p + 1) * PAIR], keys)
                scores[c, p] = jnp.where(causal, both, 0.0).astype(BF16)
        for c in range(PER):
            row = b * PER + c
            chunk = slice(row * ROW, (row + 1) * ROW)
            for p in range(HEADS // 2):
                low, high = D + 2 * p * HEAD, D + (2 * p + 1) * HEAD
                values = diagonal(kv[chunk, low:low + HEAD], kv[chunk, high:high + HEAD])
                att[row, :, p * PAIR:(p + 1) * PAIR] = dot(scores[c, p], values)

    def within_device(start, stop):
        for b in range(start, stop):
            if b < blocks:
                inputs(b)
            if b > 0:
                local(b - 1)

    cut_one = blocks // 2
    cut_two = blocks - 2
    within_device(0, cut_one)

    def later_copy(t, j):
        return remote(
            quad_send.at[part_rows(j)], quad_recv.at[t - 1, part_rows(j)],
            s2.at[t - 1, j], r2.at[t - 1, j],
            ((quad + t) % quads) * 2 + side, narrow,
        )

    for j in range(PARTS):
        piece = slice(j * PART, (j + 1) * PART)
        for t in range(1, members):
            gather_copy(t, j).wait_recv()
        quad_sum = own_total[place, piece].astype(F32)
        for t in range(1, members):
            quad_sum = quad_sum + quad_parts[t - 1, piece].astype(F32)
        quad_send[piece] = quad_sum.astype(BF16)
        for t in range(1, quads):
            @pl.when(quad + t < quads)
            def _(t=t, j=j):
                later_copy(t, j).start()

    within_device(cut_one, cut_two)
    loads[1].wait()
    mixed[...] = dot(wout[...], wfeat[...]).astype(BF16)

    def assign(b, carry):
        held = [jnp.int32(-1)] * most
        for r in range(rows):
            hit = brick_ref[0, r] == b
            held = [
                jnp.where(hit, jnp.int32(r) if m == 0 else held[m - 1], held[m]) for m in range(most)
            ]
        for m in range(most):
            slots[b * most + m] = held[m]
        return carry

    lax.fori_loop(0, wide_count, assign, 0)

    def spread_copy(t, j):
        other, to_wide, to_narrow = member(t)
        return remote(
            prefix_send.at[other, part_rows(j)], prefix_recv.at[place, part_rows(j)],
            s3.at[t - 1, j], r3.at[t - 1, j], to_wide, to_narrow,
        )

    def spread_arrival(t, j):
        source = (place - t + members) % members
        return remote(
            prefix_send.at[source, part_rows(j)], prefix_recv.at[source, part_rows(j)],
            s3.at[t - 1, j], r3.at[t - 1, j], wide, narrow,
        )

    for j in range(PARTS):
        piece = slice(j * PART, (j + 1) * PART)
        base[piece] = jnp.zeros((PART, HEAD), F32)
        for t in range(1, quads):
            @pl.when(quad - t >= 0)
            def _(t=t, j=j, piece=piece):
                later_copy(t, j).wait_recv()
                base[piece] = base[piece] + quad_recv[t - 1, piece].astype(F32)
        running = base[piece]
        for m in range(members):
            prefix_send[m, piece] = running.astype(BF16)
            if m < members - 1:
                value = own_total[place, piece].astype(F32)
                for t in range(1, members):
                    value = jnp.where(
                        (place - t + members) % members == m,
                        quad_parts[t - 1, piece].astype(F32), value,
                    )
                running = running + value
        for t in range(1, members):
            spread_copy(t, j).start()
        prefix_recv[place, piece] = prefix_send[place, piece]

    within_device(cut_two, blocks + 1)

    cell_ids = lax.broadcasted_iota(jnp.int32, (CELLS, ROW), 0)

    def across(r):
        target = wide
        for s in range(bits):
            target = target + (r // 2**s) % 2 * 2**s * (1 - 2 * ((wide // 2**s) % 2))
        return target

    def named_rows(brick):
        marks, chosen = [], []
        for m in range(most):
            named = slots[brick * most + m]
            row = jnp.maximum(named, 0)
            cells = cell_ref[pl.ds(row, 1), :] + jnp.where(named < 0, -CELLS, 0)
            marks.append(jnp.where(cell_ids == cells, 1.0, 0.0).astype(BF16))
            chosen.append(row)
        return jnp.concatenate(marks, axis=1), chosen

    early[...] = named_rows(across(wide_count - 1))[0]

    for j in range(PARTS):
        for t in range(1, members):
            spread_arrival(t, j).wait_recv()
    for h in range(HEADS):
        total[h] = prefix_recv[h].astype(F32)

    def state_of(row, p):
        return diagonal(*[
            (within[row, 2 * p + i].astype(F32) + total[2 * p + i]).astype(BF16) for i in range(2)
        ])

    def scaled(one):
        square = jnp.mean(one * one, axis=-1, keepdims=True)
        return (one * lax.rsqrt(square + epsilon)).astype(BF16)

    def attend(b):
        for row in range(PER * b, PER * (b + 1)):
            for p in range(HEADS // 2):
                columns = slice(p * PAIR, (p + 1) * PAIR)
                att[row, :, columns] += dot(qs[row, :, columns], state_of(row, p))

    def normalise(b):
        for row in range(PER * b, PER * (b + 1)):
            for h in range(HEADS):
                mine = slice(h * HEAD, (h + 1) * HEAD)
                qs[row, :, mine] = scaled(att[row, :, mine])

    def finish(b):
        span = slice(PER * b, PER * (b + 1))
        normed = qs[span].reshape(BLK, D)
        mine = direct[span].reshape(BLK, PF) + dot(normed, mixed[...])
        feats[span] = mine.astype(BF16).reshape(PER, ROW, PF)

    def project():
        for b in range(blocks + 2):
            if b < blocks:
                attend(b)
            if 0 < b <= blocks:
                normalise(b - 1)
            if b > 1:
                finish(b - 2)

    def pool_ready(brick):
        marks, chosen = named_rows(brick)
        return dot(marks, jnp.concatenate([feats[row] for row in chosen], axis=0))

    def pool_afresh(brick):
        chosen = named_rows(brick)[1]
        normed, plain = [], []
        for row in chosen:
            pieces = []
            for p in range(HEADS // 2):
                columns = slice(p * PAIR, (p + 1) * PAIR)
                attended = att[row, :, columns] + dot(qs[row, :, columns], state_of(row, p))
                pieces += [scaled(attended[:, i * HEAD:(i + 1) * HEAD]) for i in range(2)]
            normed.append(jnp.concatenate(pieces, axis=1))
            plain.append(direct[row])
        features = jnp.concatenate(plain, axis=0) + dot(jnp.concatenate(normed, axis=0), mixed[...])
        return dot(early[...], features.astype(BF16))

    def piece_copy(label, bit, k):
        span = pl.ds(k * PIECE, PIECE)
        return remote(
            part_send.at[label - 1, span], part_recv.at[label - 1, span],
            sa.at[label - 1, k], ra.at[label - 1, k], across(bit), narrow,
        )

    def send_partner(label, pool):
        part_send[label - 1] = pool.astype(BF16)
        for k in PIECE_ORDER:
            piece_copy(label, 1, k).start()

    def halo_copy(k, dy, dx):
        if dy == 0:
            source = pooled.at[:, pl.ds(BY - EDGE if dx > 0 else 0, EDGE)]
            target = cols_recv.at[0 if dx > 0 else 1]
        else:
            span = pl.ds(BX - HALO if dy > 0 else 0, HALO)
            if dx == 0:
                source = pooled.at[span]
                target = rows_recv.at[0 if dy > 0 else 1]
            else:
                source = pooled.at[span, pl.ds(BY - EDGE if dx > 0 else 0, EDGE)]
                target = corner_recv.at[(0 if dy > 0 else 2) + (0 if dx > 0 else 1)]
        return remote(
            source, target, sh.at[k], rh.at[k],
            (wide + dy + wide_count) % wide_count, (narrow + dx + narrow_count) % narrow_count,
        )

    steps = [(dy, dx) for dy in (-1, 1) for dx in (0, -1, 1)] + [(0, -1), (0, 1)]

    def inside(dy, dx):
        return (
            (wide + dy >= 0) & (wide + dy < wide_count)
            & (narrow + dx >= 0) & (narrow + dx < narrow_count)
        )

    def send_halo(wanted):
        for k, (dy, dx) in enumerate(steps):
            if dy != wanted:
                continue

            @pl.when(inside(dy, dx))
            def _(k=k, dy=dy, dx=dx):
                halo_copy(k, dy, dx).start()

    def pool_own(label):
        own_part[label // 2] = pool_ready(across(label))

    def reduce(label):
        low = label & -label if label else wide_count
        for k in PIECE_ORDER:
            span = slice(k * PIECE, (k + 1) * PIECE)
            summed = own_part[label // 2, span]
            bit = 1
            while bit < low:
                piece_copy(label + bit, bit, k).wait_recv()
                summed = summed + part_recv[label + bit - 1, span].astype(F32)
                bit *= 2
            if label:
                part_send[label - 1, span] = summed.astype(BF16)
                piece_copy(label, low, k).start()
            else:
                lines = slice(k * PIECE // BY, (k + 1) * PIECE // BY)
                done = summed.astype(BF16).reshape(PIECE // BY, BY, PF)
                pooled[lines] = done
                ext[HALO + lines.start:HALO + lines.stop, EDGE:EDGE + BY, :] = done
                if k == 0:
                    send_halo(-1)
                if k == PIECES - 1:
                    send_halo(1)

    top = wide_count - 1
    send_partner(top, pool_afresh(across(top)))
    project()
    send_partner(top - 2, pool_ready(across(top - 2)))
    pool_own(top - 1)
    reduce(top - 1)
    for label in range(top - 4, 0, -2):
        send_partner(label, pool_ready(across(label)))
    for label in range(top - 3, -1, -2):
        pool_own(label)
    for label in range(top - 3, -1, -2):
        reduce(label)
    send_halo(0)

    def take_halo(across_rows):
        for k, (dy, dx) in enumerate(steps):
            if (dy != 0) != across_rows:
                continue

            @pl.when(inside(-dy, -dx))
            def _(k=k, dy=dy, dx=dx):
                halo_copy(k, dy, dx).wait_recv()
                span = slice(HALO, HALO + BX)
                if dy > 0:
                    span = slice(0, HALO)
                elif dy < 0:
                    span = slice(HALO + BX, 2 * HALO + BX)
                if dx == 0:
                    ext[span, EDGE:EDGE + BY, :] = rows_recv[0 if dy > 0 else 1]
                else:
                    columns = slice(0, EDGE) if dx > 0 else slice(EDGE + BY, WIDTH)
                    if dy == 0:
                        ext[span, columns, :] = cols_recv[0 if dx > 0 else 1]
                    else:
                        ext[span, columns, :] = corner_recv[(0 if dy > 0 else 2) + (0 if dx > 0 else 1)]

    def convolve(field, weight, start, height):
        size = height * WIDTH
        result = None
        for dx in range(3):
            shifted = None
            for dy in range(3):
                window = field[start + dy:start + dy + height].reshape(size, PF)
                term = dot(window, weight[dy, dx])
                shifted = term if shifted is None else shifted + term
            if dx != 1:
                shifted = pltpu.roll(shifted, 1 if dx == 0 else size - 1, 0)
            result = shifted if result is None else result + shifted
        return result.reshape(height, WIDTH, PF)

    def first_layer(start, height):
        active = jax.nn.gelu(convolve(ext, first, start, height), approximate=True)
        extent = (height, WIDTH, PF)
        grid_row = lax.broadcasted_iota(jnp.int32, extent, 0) + wide * BX + start - 1
        grid_column = lax.broadcasted_iota(jnp.int32, extent, 1) + narrow * BY - EDGE
        real = (
            (grid_row >= 0) & (grid_row < wide_count * BX)
            & (grid_column >= 0) & (grid_column < narrow_count * BY)
        )
        inner[start:start + height] = jnp.where(real, active, 0.0).astype(BF16)

    def second_layer(start, height):
        out_ref[start:start + height] = convolve(inner, second, start, height)[:, EDGE:EDGE + BY, :]

    loads[3].wait()
    loads[4].wait()
    take_halo(False)
    first_layer(HALO, BX - HALO)
    second_layer(HALO, BX - 2 * HALO)
    take_halo(True)
    first_layer(0, HALO)
    first_layer(BX, HALO)
    second_layer(0, HALO)
    second_layer(BX - HALO, HALO)

    for j in range(PARTS):
        for t in range(1, members):
            gather_copy(t, j).wait_send()
            spread_copy(t, j).wait_send()
        for t in range(1, quads):
            @pl.when(quad + t < quads)
            def _(t=t, j=j):
                later_copy(t, j).wait_send()

    for label in range(1, wide_count):
        for k in range(PIECES):
            piece_copy(label, label & -label, k).wait_send()
    for k, (dy, dx) in enumerate(steps):
        @pl.when(inside(dy, dx))
        def _(k=k, dy=dy, dx=dx):
            halo_copy(k, dy, dx).wait_send()


def per_device(voxels, w_qkv, w_out, w_feature, conv_first, conv_second, row_brick, cell_place):
    token_count = voxels.shape[0]
    rows = token_count // ROW
    wide_count = lax.axis_size("wide")
    narrow_count = lax.axis_size("narrow")
    blocks = token_count // BLK
    quads = wide_count // 2
    members = 2 * narrow_count
    others = max(1, quads - 1)
    most = 2 * (-(-rows // wide_count))
    anywhere = pl.BlockSpec(memory_space=pl.ANY)
    vmem = pl.BlockSpec(memory_space=pltpu.VMEM)
    smem = pl.BlockSpec(memory_space=pltpu.SMEM)
    dma = pltpu.SemaphoreType.DMA
    state = (HEAD, HEAD)
    grid = (CELLS, PF)
    scratch = [
        pltpu.VMEM(voxels.shape, BF16),
        pltpu.VMEM(w_qkv.shape, BF16),
        pltpu.VMEM(w_out.shape, BF16),
        pltpu.VMEM(w_feature.shape, BF16),
        pltpu.VMEM(conv_first.shape, BF16),
        pltpu.VMEM(conv_second.shape, BF16),
        pltpu.VMEM((token_count, 2 * D), BF16),
        pltpu.VMEM((rows, ROW, D), BF16),
        pltpu.VMEM((rows, ROW, D), F32),
        pltpu.VMEM((rows, ROW, PF), F32),
        pltpu.VMEM((D, PF), BF16),
        pltpu.VMEM((rows, HEADS) + state, BF16),
        pltpu.VMEM((HEADS,) + state, F32),
        pltpu.VMEM((rows, ROW, PF), BF16),
        pltpu.SMEM((wide_count * most,), jnp.int32),
        pltpu.VMEM((MIDDLE, D), F32),
        pltpu.VMEM((MIDDLE, MIDDLE), F32),
        pltpu.VMEM((D, D), BF16),
        pltpu.VMEM(state, F32),
        pltpu.VMEM((CELLS, most * ROW), BF16),
        pltpu.VMEM((members,) + state, BF16),
        pltpu.VMEM((members,) + state, BF16),
        pltpu.VMEM(state, BF16),
        pltpu.VMEM((others,) + state, BF16),
        pltpu.VMEM((members,) + state, BF16),
        pltpu.VMEM((members,) + state, BF16),
        pltpu.VMEM((wide_count - 1,) + grid, BF16),
        pltpu.VMEM((wide_count - 1,) + grid, BF16),
        pltpu.VMEM((quads,) + grid, F32),
        pltpu.VMEM((BX, BY, PF), BF16),
        pltpu.VMEM((BX + 2 * HALO, WIDTH, PF), BF16),
        pltpu.VMEM((2, HALO, BY, PF), BF16),
        pltpu.VMEM((2, BX, EDGE, PF), BF16),
        pltpu.VMEM((4, HALO, EDGE, PF), BF16),
        pltpu.VMEM((BX + 2, WIDTH, PF), BF16),
        dma((blocks,)),
        dma((6,)),
        dma((members - 1, PARTS)), dma((members - 1, PARTS)),
        dma((others, PARTS)), dma((others, PARTS)),
        dma((members - 1, PARTS)), dma((members - 1, PARTS)),
        dma((wide_count - 1, PIECES)), dma((wide_count - 1, PIECES)),
        dma((8,)), dma((8,)),
    ]
    return pl.pallas_call(
        functools.partial(kernel, wide_count, narrow_count, token_count, most),
        out_shape=jax.ShapeDtypeStruct((BX, BY, PF), F32),
        in_specs=[anywhere] * 6 + [smem, vmem],
        out_specs=vmem,
        scratch_shapes=scratch,
        compiler_params=pltpu.CompilerParams(
            collective_id=0, has_side_effects=True, vmem_limit_bytes=56 * 1024 * 1024
        ),
        name="scene_flow",
    )(
        voxels, w_qkv, w_out, w_feature, conv_first, conv_second,
        row_brick.reshape(1, rows), cell_place.reshape(rows, ROW),
    )


def solution(mesh):
    placed = (
        P(("group", "wide", "narrow"), None),
        P(),
        P(),
        P(),
        P(),
        P(),
        P(("group", "wide", "narrow"), None),
        P(("group", "wide", "narrow")),
    )
    return jax.shard_map(
        per_device,
        mesh=mesh,
        in_specs=placed,
        out_specs=P(("group", "wide"), "narrow", None),
        check_vma=False,
    )
```
